32 devices in a mesh: dp: 4 (over x, core), ctx: 8 (over z, y).
Axes of the slice: x: 2, y: 2, z: 4, core: 2. Of those that a mesh axis runs over, the one named last changes fastest.
Arguments:
- hidden_in: bfloat16 [8192, 1024], P(('dp', 'ctx')), may hold values from -6 to 6
- segment_ids: int32 [4, 1, 2048], P('dp'), may hold values from 0 to 15, as said below
- query_weight: float32 [2, 1024, 1024], P(None, 'ctx'), may hold values from -0.1875 to 0.1875
- query_bias: float32 [2, 1024], P(None, 'ctx'), may hold values from -3 to 3
- key_weight: float32 [2, 1024, 1024], P(None, 'ctx'), may hold values from -0.1875 to 0.1875
- value_weight: float32 [2, 1024, 1024], P(None, 'ctx'), may hold values from -0.1875 to 0.1875
- value_bias: float32 [2, 1024], P(None, 'ctx'), may hold values from -3 to 3
- output_weight: float32 [2, 1024, 1024], P(None, 'ctx'), may hold values from -0.5 to 0.5
- output_bias: float32 [2, 1024], P(None, 'ctx'), may hold values from -3 to 3
- first_gain: float32 [2, 1024], P(None, 'ctx'), may hold values from 0.5 to 1.5
- first_shift: float32 [2, 1024], P(None, 'ctx'), may hold values from -2 to 2
- inner_weight: float32 [2, 1024, 4096], P(None, 'ctx'), may hold values from -0.1875 to 0.1875
- inner_bias: float32 [2, 4096], P(None, 'ctx'), may hold values from -3 to 3
- outer_weight: float32 [2, 4096, 1024], P(None, 'ctx'), may hold values from -0.09375 to 0.09375
- outer_bias: float32 [2, 1024], P(None, 'ctx'), may hold values from -2 to 2
- second_gain: float32 [2, 1024], P(None, 'ctx'), may hold values from 0.5 to 1.5
- second_shift: float32 [2, 1024], P(None, 'ctx'), may hold values from -2 to 2
- cotangent: bfloat16 [8192, 1024], P(('dp', 'ctx')), may hold values from -6 to 6
Outputs:
- output: bfloat16 [8192, 1024], P(('dp', 'ctx'))
- input_gradient: bfloat16 [8192, 1024], P(('dp', 'ctx'))
- query_weight_gradient: float32 [2, 1024, 1024], P(None, 'ctx')
- query_bias_gradient: float32 [2, 1024], P(None, 'ctx')
- key_weight_gradient: float32 [2, 1024, 1024], P(None, 'ctx')
- value_weight_gradient: float32 [2, 1024, 1024], P(None, 'ctx')
- value_bias_gradient: float32 [2, 1024], P(None, 'ctx')
- output_weight_gradient: float32 [2, 1024, 1024], P(None, 'ctx')
- output_bias_gradient: float32 [2, 1024], P(None, 'ctx')
- first_gain_gradient: float32 [2, 1024], P(None, 'ctx')
- first_shift_gradient: float32 [2, 1024], P(None, 'ctx')
- inner_weight_gradient: float32 [2, 1024, 4096], P(None, 'ctx')
- inner_bias_gradient: float32 [2, 4096], P(None, 'ctx')
- outer_weight_gradient: float32 [2, 4096, 1024], P(None, 'ctx')
- outer_bias_gradient: float32 [2, 1024], P(None, 'ctx')
- second_gain_gradient: float32 [2, 1024], P(None, 'ctx')
- second_shift_gradient: float32 [2, 1024], P(None, 'ctx')
The draws below stay inside these ranges and needn't reach their ends.
Inputs may be any that keep to these rules, and one draw needn't show every extreme that they name: `segment_ids`: within each sequence of 2048 tokens (a row of the last dimension) the numbers never fall, every number 0 .. 15 is used, and each document has 1 to 512 tokens, one exactly 512.
All inputs are finite; a program needn't handle non-finite values.
Results may differ from the reference program's by a relative error of at most 0.025.
Values may be sent and summed in bfloat16 or wider, within the bound.
No kernel may reach another device: no remote copies, remote signals or barrier semaphores. Data moves between devices by JAX's collectives and lax.ppermute only.
A program may use at most 256 MiB of HBM per device.

```python
import jax
import jax.numpy as jnp
from jax import lax

D = 1024
HEADS = 16
HD = 64
FF = 4096
LAYERS = 2
SEQ = 2048
MAXDOC = 512
DOCS = 16
TOK_DEV = 256
SEQS_GROUP = 1
TOKENS = 8192
N_DP = 4


def sequence_lengths(key, odd_turn):
    half_docs = DOCS // 2
    short_most = max(1, min(TOK_DEV - 1, MAXDOC) // DOCS)
    short_count = half_docs if odd_turn else DOCS - 1 - half_docs
    long_count = DOCS - short_count
    free_count = long_count - 1
    short_key, share_key, shift_key, place_key = jax.random.split(key, 4)
    short_sizes = jax.random.randint(short_key, (short_count,), 1, short_most + 1, dtype=jnp.int32)
    shares = jnp.right_shift(jax.random.randint(share_key, (free_count,), 0, 1025, dtype=jnp.int32), jax.random.randint(shift_key, (free_count,), 0, 5, dtype=jnp.int32))
    remaining = SEQ - MAXDOC - jnp.sum(short_sizes)
    free_sizes = []
    for position in range(free_count):
        later_docs = free_count - 1 - position
        lowest = jnp.maximum(1, remaining - later_docs * MAXDOC)
        highest = jnp.minimum(MAXDOC, remaining - later_docs)
        length = lowest + (highest - lowest) * shares[position] // 1024
        free_sizes.append(length)
        remaining = remaining - length
    free_sizes = jnp.stack(free_sizes).astype(jnp.int32)
    forced = jax.random.randint(place_key, (), 0, long_count, dtype=jnp.int32)
    places = jnp.arange(long_count, dtype=jnp.int32)
    empty_slot = jnp.zeros((1,), jnp.int32)
    long_sizes = jnp.where(places < forced, jnp.concatenate([free_sizes, empty_slot]), jnp.where(places == forced, MAXDOC, jnp.concatenate([empty_slot, free_sizes])))
    if odd_turn:
        doc_sizes = jnp.concatenate([short_sizes, long_sizes.astype(jnp.int32)])
    else:
        doc_sizes = jnp.concatenate([long_sizes.astype(jnp.int32), short_sizes])
    return doc_sizes


def draw_segment_ids(key, part):
    sequences = []
    token_places = jnp.arange(SEQ, dtype=jnp.int32)
    for position in range(N_DP * SEQS_GROUP):
        doc_sizes = sequence_lengths(jax.random.fold_in(key, position), position % SEQS_GROUP % 2 == 1)
        doc_ends = jnp.cumsum(doc_sizes).astype(jnp.int32)
        passed = (token_places[:, None] >= doc_ends[None, :DOCS - 1]).astype(jnp.int32)
        sequences.append(jnp.sum(passed, axis=1).astype(jnp.int32))
    return jnp.stack(sequences).reshape(N_DP, SEQS_GROUP, SEQ).astype(jnp.int32)


def block_levels(own_key, extent, cuts, least, top_value):
    level = 1.0
    for dim, blocks in cuts:
        steps = jax.random.uniform(jax.random.fold_in(jax.random.fold_in(own_key, 6), dim), (blocks,), jnp.float32, least / len(cuts), top_value / len(cuts))
        level = level * jnp.repeat(jnp.exp(steps), extent[dim] // blocks).reshape((-1,) + (1,) * (len(extent) - 1 - dim))
    return level


def gaussian(own_key, extent, deviation, most, pieces=(), kind=jnp.bfloat16):
    level = block_levels(own_key, extent, pieces, -0.22, 0.18) if pieces else 1.0
    entries = jax.random.normal(own_key, extent, jnp.float32) * deviation * level
    return jnp.minimum(jnp.maximum(entries, -most), most).astype(kind)


def setup_inputs(seed: int = 0) -> dict:
    streams_of = jax.random.split(jax.random.key(seed), 19)
    return {
        "hidden_in": gaussian(streams_of[0], (TOKENS, D), 1.0, 6.0, ((0, 32),)),
        "segment_ids": draw_segment_ids(jax.random.fold_in(streams_of[18], 71), 0),
        "query_weight": gaussian(streams_of[2], (LAYERS, D, D), D ** -0.5, 0.1875, ((1, 8),), jnp.float32),
        "query_bias": gaussian(streams_of[3], (LAYERS, D), 0.5, 3.0, ((1, 8),), jnp.float32),
        "key_weight": gaussian(streams_of[4], (LAYERS, D, D), D ** -0.5, 0.1875, ((1, 8),), jnp.float32),
        "value_weight": gaussian(streams_of[5], (LAYERS, D, D), D ** -0.5, 0.1875, ((1, 8),), jnp.float32),
        "value_bias": gaussian(streams_of[6], (LAYERS, D), 0.5, 3.0, ((1, 8),), jnp.float32),
        "output_weight": gaussian(streams_of[7], (LAYERS, D, D), (D // 8) ** -0.5, 0.5, ((1, 8),), jnp.float32),
        "output_bias": gaussian(streams_of[8], (LAYERS, D), 0.5, 3.0, ((1, 8),), jnp.float32),
        "first_gain": jnp.clip(1.0 + 0.1 * jax.random.normal(streams_of[9], (LAYERS, D), jnp.float32), 0.5, 1.5),
        "first_shift": gaussian(streams_of[10], (LAYERS, D), 0.3, 2.0, ((1, 8),), jnp.float32),
        "inner_weight": gaussian(streams_of[11], (LAYERS, D, FF), D ** -0.5, 0.1875, ((1, 8),), jnp.float32),
        "inner_bias": gaussian(streams_of[12], (LAYERS, FF), 0.5, 3.0, ((1, 8),), jnp.float32),
        "outer_weight": gaussian(streams_of[13], (LAYERS, FF, D), FF ** -0.5, 0.09375, ((1, 8),), jnp.float32),
        "outer_bias": gaussian(streams_of[14], (LAYERS, D), 0.3, 2.0, ((1, 8),), jnp.float32),
        "second_gain": jnp.clip(1.0 + 0.1 * jax.random.normal(streams_of[15], (LAYERS, D), jnp.float32), 0.5, 1.5),
        "second_shift": gaussian(streams_of[16], (LAYERS, D), 0.3, 2.0, ((1, 8),), jnp.float32),
        "cotangent": gaussian(streams_of[17], (TOKENS, D), 1.0, 6.0, ((0, 32),)),
    }


@jax.custom_vjp
def low(v):
    return lax.optimization_barrier(v.astype(jnp.bfloat16)).astype(jnp.float32)

@jax.custom_vjp
def low_back(v):
    return v

def low_keep(v):
    return (low(v), None)

def low_pass(kept, grad):
    return (grad,)

def back_keep(v):
    return (v, None)

def back_low(kept, grad):
    return (low(grad),)
low.defvjp(low_keep, low_pass)
low_back.defvjp(back_keep, back_low)

def matmul(left, right):
    return jnp.dot(left, right, precision=lax.Precision.HIGHEST)

def both_ways(operand):
    return low(low_back(operand))

def normalize(operand, norm_gain, norm_shift):
    centered = operand - lax.optimization_barrier(jnp.mean(operand, axis=-1, keepdims=True))
    spread = lax.optimization_barrier(jnp.mean(centered * centered, axis=-1, keepdims=True))
    return centered * lax.rsqrt(spread + 1e-05) * norm_gain + norm_shift

def head_attend(query_rows, key_rows, value_rows, same_document):
    scores = low_back(matmul(query_rows, key_rows.T))
    scores = jnp.where(same_document, scores, -1e+30)
    row_top = lax.optimization_barrier(jnp.max(scores, axis=-1, keepdims=True))
    exponent = jnp.exp(scores - row_top)
    probabilities = exponent / lax.optimization_barrier(jnp.sum(exponent, axis=-1, keepdims=True))
    return matmul(low(probabilities), value_rows)

def attention(query_rows, key_rows, value_rows, same_document):

    def split_heads(operand):
        return jnp.transpose(operand.reshape(SEQ, HEADS, HD), (1, 0, 2))

    def one_head(triple):
        return head_attend(triple[0], triple[1], triple[2], same_document)
    mixed_heads = lax.map(jax.checkpoint(one_head), (split_heads(query_rows), split_heads(key_rows), split_heads(value_rows)))
    return jnp.transpose(mixed_heads, (1, 0, 2)).reshape(SEQ, D)

def encoder(params, hidden, segment_row):
    same_document = segment_row[:, None] == segment_row[None, :]
    score_scale = HD ** (-0.5)
    for layer_index in range(LAYERS):
        query_weight, query_bias, key_weight, value_weight, value_bias, output_weight, output_bias, first_gain, first_shift, inner_weight, inner_bias, outer_weight, outer_bias, second_gain, second_shift = [low(param[layer_index]) for param in params]
        rounded = low(hidden)
        query_rows = both_ways((matmul(rounded, query_weight) + query_bias) * score_scale)
        key_rows = both_ways(matmul(rounded, key_weight))
        value_rows = both_ways(matmul(rounded, value_weight) + value_bias)
        mixed_heads = both_ways(attention(query_rows, key_rows, value_rows, same_document))
        branch = low_back(matmul(mixed_heads, output_weight) + output_bias)
        settled = normalize(hidden + branch, first_gain, first_shift)
        inner_act = low_back(matmul(low(settled), inner_weight) + inner_bias)
        activated = low(jax.nn.gelu(inner_act, approximate=False))
        outer_act = low_back(matmul(activated, outer_weight) + outer_bias)
        hidden = normalize(settled + outer_act, second_gain, second_shift)
    return hidden

def reference(hidden_in, segment_ids, query_weight, query_bias, key_weight, value_weight, value_bias, output_weight, output_bias, first_gain, first_shift, inner_weight, inner_bias, outer_weight, outer_bias, second_gain, second_shift, cotangent):
    params = tuple((param.astype(jnp.float32) for param in (query_weight, query_bias, key_weight, value_weight, value_bias, output_weight, output_bias, first_gain, first_shift, inner_weight, inner_bias, outer_weight, outer_bias, second_gain, second_shift)))
    inputs = hidden_in.astype(jnp.float32).reshape(-1, SEQ, D)
    segment_rows = segment_ids.reshape(-1, SEQ)
    cotangents = cotangent.astype(jnp.float32).reshape(-1, SEQ, D)

    def one_sequence(totals, portion):
        sequence_in, sequence_ids, sequence_cot = portion
        result, pullback = jax.vjp(lambda weights, given_rows: encoder(weights, given_rows, sequence_ids), params, sequence_in)
        weight_grads, input_grad = pullback(sequence_cot)
        totals = tuple((running + gradient for running, gradient in zip(totals, weight_grads)))
        return (totals, (result, input_grad))
    zeros = tuple((jnp.zeros_like(param) for param in params))
    totals, (results, input_grads) = lax.scan(one_sequence, zeros, (inputs, segment_rows, cotangents))
    return (results.reshape(-1, D).astype(jnp.bfloat16), input_grads.reshape(-1, D).astype(jnp.bfloat16), totals[0], totals[1], totals[2], totals[3], totals[4], totals[5], totals[6], totals[7], totals[8], totals[9], totals[10], totals[11], totals[12], totals[13], totals[14])
```

```python
import jax
import jax.numpy as jnp
from jax import lax
from jax.experimental import pallas as pl
from jax.experimental.pallas import tpu as pltpu
from jax.sharding import PartitionSpec as P

HD = 64
LAYERS = 2
SEQ = 2048
SLOTS = 5
OWN = 2
BF16 = jnp.bfloat16
F32 = jnp.float32
CORE_PAIRS = [(i, i ^ 1) for i in range(4)]
X_PAIRS = [(i, i ^ 2) for i in range(4)]


def dot(left, right, dims, out=F32):
    return lax.dot_general(left, right, (dims, ((), ())), preferred_element_type=F32).astype(out)


NN = ((1,), (0,))
NT = ((1,), (1,))
TN = ((0,), (0,))


def core_swap(value):
    return lax.ppermute(value, "dp", CORE_PAIRS)


def x_swap(value):
    return lax.ppermute(value, "dp", X_PAIRS)


def tie(value, *tokens):
    return lax.optimization_barrier((value,) + tokens)[0]


def ordered(place, mine, peer, axis):
    first = jnp.where(place == 0, mine, peer)
    second = jnp.where(place == 0, peer, mine)
    return jnp.concatenate([first, second], axis=axis)


class Ring:
    def __init__(self, n):
        self.n = n
        self.order = [2 * r if r < n // 2 else 2 * (n - 1 - r) + 1 for r in range(n)]
        self.cw = [(self.order[r], self.order[(r + 1) % n]) for r in range(n)]
        self.ccw = [(b, a) for a, b in self.cw]
        ctx = lax.axis_index("ctx")
        self.place = jnp.where(ctx % 2 == 0, ctx // 2, n - 1 - ctx // 2)

    def member(self, distance):
        r = (self.place + distance) % self.n
        return jnp.where(r < self.n // 2, 2 * r, 2 * (self.n - 1 - r) + 1)

    def gather(self, own, long_cw):
        n = self.n
        chunks, distances = [own], [0]
        forward, backward = own, own
        cw_steps = n // 2 if long_cw else n // 2 - 1
        for step in range(1, n // 2 + 1):
            if step <= cw_steps:
                forward = lax.ppermute(forward, "ctx", self.cw)
                chunks.append(forward)
                distances.append(-step)
            if step <= n - 1 - cw_steps:
                backward = lax.ppermute(backward, "ctx", self.ccw)
                chunks.append(backward)
                distances.append(step)
        return chunks, distances

    def scatter(self, part_of, long_cw):
        n = self.n
        cw_steps = n // 2 if long_cw else n // 2 - 1
        ccw_steps = n - 1 - cw_steps
        got_cw = got_ccw = None
        for step in range(n // 2, 0, -1):
            if step <= cw_steps:
                part = part_of(self.member(step))
                if got_cw is not None:
                    part = part + got_cw.astype(F32)
                got_cw = lax.ppermute(part.astype(BF16), "ctx", self.cw)
            if step <= ccw_steps:
                part = part_of(self.member(-step))
                if got_ccw is not None:
                    part = part + got_ccw.astype(F32)
                got_ccw = lax.ppermute(part.astype(BF16), "ctx", self.ccw)
        return part_of(lax.axis_index("ctx")) + got_cw.astype(F32) + got_ccw.astype(F32)


def assemble_attention(chunks, owners):
    n = len(chunks)
    rows, wide = chunks[0].shape
    w = wide // 4

    def kernel(owner_ref, *refs):
        ins, qkv_ref, out_ref, sems = refs[:n], refs[n], refs[n + 1], refs[n + 2]
        copies = []
        for i in range(n):
            o = owner_ref[i]
            copies.append(pltpu.make_async_copy(ins[i].at[:, : 3 * w], qkv_ref.at[o], sems.at[2 * i]))
            copies.append(pltpu.make_async_copy(ins[i].at[:, 3 * w :], out_ref.at[o], sems.at[2 * i + 1]))
        for c in copies:
            c.start()
        for c in copies:
            c.wait()

    return pl.pallas_call(
        kernel,
        out_shape=(
            jax.ShapeDtypeStruct((n, rows, 3 * w), BF16),
            jax.ShapeDtypeStruct((n, rows, w), BF16),
        ),
        in_specs=[pl.BlockSpec(memory_space=pltpu.SMEM)] + [pl.BlockSpec(memory_space=pl.ANY)] * n,
        out_specs=(pl.BlockSpec(memory_space=pl.ANY), pl.BlockSpec(memory_space=pl.ANY)),
        scratch_shapes=[pltpu.SemaphoreType.DMA((2 * n,))],
    )(owners, *chunks)


def assemble_feed(mine, other, owners, place):
    n = len(mine)
    both, cols = mine[0].shape
    rows = both // 2

    def kernel(owner_ref, place_ref, *refs):
        ins, first_ref, second_ref, sems = refs[: 2 * n], refs[2 * n], refs[2 * n + 1], refs[2 * n + 2]
        copies = []
        for half in range(2):
            for i in range(n):
                o = owner_ref[i]
                h = place_ref[half]
                src = ins[half * n + i]
                k = 2 * (half * n + i)
                col = pl.multiple_of(h * cols, 128)
                copies.append(
                    pltpu.make_async_copy(
                        src.at[:rows], first_ref.at[o, :, pl.ds(col, cols)], sems.at[k]
                    )
                )
                copies.append(
                    pltpu.make_async_copy(src.at[rows:], second_ref.at[h, o], sems.at[k + 1])
                )
        for c in copies:
            c.start()
        for c in copies:
            c.wait()

    return pl.pallas_call(
        kernel,
        out_shape=(
            jax.ShapeDtypeStruct((n, rows, 2 * cols), BF16),
            jax.ShapeDtypeStruct((2, n, rows, cols), BF16),
        ),
        in_specs=[pl.BlockSpec(memory_space=pltpu.SMEM)] * 2 + [pl.BlockSpec(memory_space=pl.ANY)] * (2 * n),
        out_specs=(pl.BlockSpec(memory_space=pl.ANY), pl.BlockSpec(memory_space=pl.ANY)),
        scratch_shapes=[pltpu.SemaphoreType.DMA((4 * n,))],
    )(owners, place, *mine, *other)


SLOT_ORDER = (2, 1, 3, 0, 4)


def attend_kernel(need_ref, q_ref, k_ref, v_ref, qseg_ref, kseg_ref, mixed_ref, lse_ref, top, total, acc):
    seq = pl.program_id(0)
    q = q_ref[0]
    tokens = q.shape[0]
    lane = lax.broadcasted_iota(jnp.int32, q.shape, 1)
    zero = jnp.zeros_like(q)
    heads = (jnp.where(lane < HD, q, zero), jnp.where(lane < HD, zero, q))
    qseg = qseg_ref[0]

    def one_slot(slot, first):
        keys = k_ref[0, slot]
        values = v_ref[0, slot]
        mask = kseg_ref[0, slot * tokens : (slot + 1) * tokens] == qseg
        for h in range(2):
            scores = dot(keys, heads[h], NT)
            scores = jnp.where(mask, scores, -1e30)
            best = jnp.max(scores, axis=0, keepdims=True)
            if not first:
                old = top[h]
                best = jnp.maximum(best, old)
            expo = jnp.exp(scores - best)
            sums = jnp.sum(expo, axis=0, keepdims=True)
            part = dot(values, expo.astype(BF16), TN)
            if not first:
                shrink = jnp.exp(old - best)
                sums = sums + total[h] * shrink
                part = part + acc[h] * shrink
            top[h] = best
            total[h] = sums
            acc[h] = part

    one_slot(OWN, True)
    for slot in SLOT_ORDER[1:]:

        @pl.when(need_ref[seq * SLOTS + slot] > 0)
        def _(slot=slot):
            one_slot(slot, False)

    halves = [acc[h][HD * h : HD * (h + 1)] / total[h] for h in range(2)]
    mixed_ref[0] = jnp.concatenate(halves, axis=0).T.astype(BF16)
    lse_ref[0, 0] = jnp.concatenate([top[h] + jnp.log(total[h]) for h in range(2)], axis=0)


def attend(queries, keys_values, query_ids, key_ids, need):
    seqs, tokens, width = queries.shape
    pairs = width // 128
    return pl.pallas_call(
        attend_kernel,
        grid_spec=pltpu.PrefetchScalarGridSpec(
            num_scalar_prefetch=1,
            grid=(seqs, pairs),
            in_specs=[
                pl.BlockSpec((1, tokens, 128), lambda s, p, n: (s, 0, p)),
                pl.BlockSpec((1, SLOTS, tokens, 128), lambda s, p, n: (s, 0, 0, p)),
                pl.BlockSpec((1, SLOTS, tokens, 128), lambda s, p, n: (s, 0, 0, pairs + p)),
                pl.BlockSpec((1, 1, tokens), lambda s, p, n: (s, 0, 0)),
                pl.BlockSpec((1, SLOTS * tokens, 1), lambda s, p, n: (s, 0, 0)),
            ],
            out_specs=[
                pl.BlockSpec((1, tokens, 128), lambda s, p, n: (s, 0, p)),
                pl.BlockSpec((1, 1, 2, tokens), lambda s, p, n: (s, p, 0, 0)),
            ],
            scratch_shapes=[
                pltpu.VMEM((2, 1, tokens), F32),
                pltpu.VMEM((2, 1, tokens), F32),
                pltpu.VMEM((2, 128, tokens), F32),
            ],
        ),
        out_shape=(
            jax.ShapeDtypeStruct((seqs, tokens, width), BF16),
            jax.ShapeDtypeStruct((seqs, pairs, 2, tokens), F32),
        ),
    )(need, queries, keys_values, keys_values, query_ids, key_ids)


def attend_back_kernel(
    need_ref, q_ref, k_ref, v_ref, g_ref, mixed_ref, lse_ref, qseg_ref, kseg_ref, gq_ref, gk_ref, gv_ref, acc
):
    seq = pl.program_id(0)
    q = q_ref[0]
    g = g_ref[0]
    tokens = q.shape[0]
    lane = lax.broadcasted_iota(jnp.int32, q.shape, 1)
    zero = jnp.zeros_like(q)
    heads = (jnp.where(lane < HD, q, zero), jnp.where(lane < HD, zero, q))
    grads = (jnp.where(lane < HD, g, zero), jnp.where(lane < HD, zero, g))
    qseg = qseg_ref[0]
    product = (g.astype(F32) * mixed_ref[0].astype(F32)).T
    inner = [jnp.sum(product[HD * h : HD * (h + 1)], axis=0, keepdims=True) for h in range(2)]
    lse = lse_ref[0, 0]

    def one_slot(slot, first):
        keys = k_ref[0, slot]
        values = v_ref[0, slot]
        mask = kseg_ref[0, slot * tokens : (slot + 1) * tokens] == qseg
        key_grad = value_grad = None
        for h in range(2):
            scores = dot(keys, heads[h], NT)
            probs = jnp.exp(jnp.where(mask, scores, -1e30) - lse[h : h + 1])
            grad_probs = dot(values, grads[h], NT)
            grad_scores = (probs * (grad_probs - inner[h])).astype(BF16)
            part = dot(keys, grad_scores, TN)
            acc[h] = part if first else acc[h] + part
            key_part = dot(grad_scores, heads[h], NN)
            value_part = dot(probs.astype(BF16), grads[h], NN)
            key_grad = key_part if h == 0 else key_grad + key_part
            value_grad = value_part if h == 0 else value_grad + value_part
        gk_ref[0, slot] = key_grad.astype(BF16)
        gv_ref[0, slot] = value_grad.astype(BF16)

    one_slot(OWN, True)
    for slot in SLOT_ORDER[1:]:
        wanted = need_ref[seq * SLOTS + slot] > 0

        @pl.when(wanted)
        def _(slot=slot):
            one_slot(slot, False)

        @pl.when(jnp.logical_not(wanted))
        def _(slot=slot):
            gk_ref[0, slot] = zero
            gv_ref[0, slot] = zero

    joined = jnp.concatenate([acc[h][HD * h : HD * (h + 1)] for h in range(2)], axis=0)
    gq_ref[0] = joined.T.astype(BF16) * (HD**-0.5)


def attend_back(queries, keys_values, grad_mixed, mixed, lse, query_ids, key_ids, need):
    seqs, tokens, width = queries.shape
    pairs = width // 128
    row_spec = pl.BlockSpec((1, tokens, 128), lambda s, p, n: (s, 0, p))
    slot_spec = pl.BlockSpec((1, SLOTS, tokens, 128), lambda s, p, n: (s, 0, 0, p))
    return pl.pallas_call(
        attend_back_kernel,
        grid_spec=pltpu.PrefetchScalarGridSpec(
            num_scalar_prefetch=1,
            grid=(seqs, pairs),
            in_specs=[
                row_spec,
                slot_spec,
                pl.BlockSpec((1, SLOTS, tokens, 128), lambda s, p, n: (s, 0, 0, pairs + p)),
                row_spec,
                row_spec,
                pl.BlockSpec((1, 1, 2, tokens), lambda s, p, n: (s, p, 0, 0)),
                pl.BlockSpec((1, 1, tokens), lambda s, p, n: (s, 0, 0)),
                pl.BlockSpec((1, SLOTS * tokens, 1), lambda s, p, n: (s, 0, 0)),
            ],
            out_specs=[row_spec, slot_spec, slot_spec],
            scratch_shapes=[pltpu.VMEM((2, 128, tokens), F32)],
        ),
        out_shape=(
            jax.ShapeDtypeStruct((seqs, tokens, width), BF16),
            jax.ShapeDtypeStruct((seqs, SLOTS, tokens, width), BF16),
            jax.ShapeDtypeStruct((seqs, SLOTS, tokens, width), BF16),
        ),
    )(need, queries, keys_values, keys_values, grad_mixed, mixed, lse, query_ids, key_ids)


def normalize(operand, gain, shift):
    centered = operand - jnp.mean(operand, axis=-1, keepdims=True)
    spread = jnp.mean(centered * centered, axis=-1, keepdims=True)
    return centered * lax.rsqrt(spread + 1e-05) * gain + shift


def normalize_back(operand, gain, grad):
    centered = operand - jnp.mean(operand, axis=-1, keepdims=True)
    spread = jnp.mean(centered * centered, axis=-1, keepdims=True)
    inverse = lax.rsqrt(spread + 1e-05)
    unit = centered * inverse
    scaled = grad * gain
    out = inverse * (
        scaled
        - jnp.mean(scaled, axis=-1, keepdims=True)
        - unit * jnp.mean(scaled * unit, axis=-1, keepdims=True)
    )
    return out, jnp.sum(grad * unit, axis=0), jnp.sum(grad, axis=0)


def column_sums(operand):
    return jnp.sum(operand.astype(F32), axis=0)


def shifts(n, by):
    return [(i, i + by) for i in range(n) if 0 <= i + by < n]


def widen(own, n):
    odd = lax.axis_index("ctx") % 2 == 1
    pairs = [(i, i ^ 1) for i in range(n)]
    behind = lax.ppermute(own, "ctx", shifts(n, 2))
    ahead = lax.ppermute(own, "ctx", shifts(n, -2))
    beside = lax.ppermute(own, "ctx", pairs)
    across = lax.ppermute(jnp.where(odd, behind, ahead), "ctx", pairs)
    return jnp.stack([behind, beside, own, across, ahead])


def give_back(parts, n):
    odd = lax.axis_index("ctx") % 2 == 1
    pairs = [(i, i ^ 1) for i in range(n)]
    across = lax.ppermute(parts[3].astype(BF16), "ctx", pairs).astype(F32)
    beside = lax.ppermute(parts[1].astype(BF16), "ctx", pairs).astype(F32)
    behind = parts[0] + jnp.where(odd, across, 0.0)
    ahead = parts[4] + jnp.where(odd, 0.0, across)
    from_ahead = lax.ppermute(behind.astype(BF16), "ctx", shifts(n, -2)).astype(F32)
    from_behind = lax.ppermute(ahead.astype(BF16), "ctx", shifts(n, 2)).astype(F32)
    return parts[2] + beside + from_ahead + from_behind


def slot_ids(group_ids, tokens, n):
    ctx = lax.axis_index("ctx")
    per = SEQ // tokens
    odd = ctx % 2 == 1
    blocks = [ctx - 2, ctx ^ 1, ctx, jnp.where(odd, ctx + 1, ctx - 1), ctx + 2]
    out = []
    for block in blocks:
        inside = (block >= 0) & (block < n) & (block // per == ctx // per)
        start = jnp.clip(block, 0, n - 1) * tokens
        out.append(jnp.where(inside, lax.dynamic_slice_in_dim(group_ids, start, tokens), -1))
    return jnp.stack(out)


def local(
    hidden_in,
    segment_ids,
    query_weight,
    query_bias,
    key_weight,
    value_weight,
    value_bias,
    output_weight,
    output_bias,
    first_gain,
    first_shift,
    inner_weight,
    inner_bias,
    outer_weight,
    outer_bias,
    second_gain,
    second_shift,
    cotangent,
):
    tokens, width = hidden_in.shape
    n = lax.axis_size("ctx")
    ctx = lax.axis_index("ctx")
    dp = lax.axis_index("dp")
    core = dp % 2
    x = dp // 2
    half = width // 2
    ff = inner_weight.shape[2]
    quarter = ff // (4 * n)
    wide = ff // 4
    scale = HD**-0.5
    ring = Ring(n)

    def attention_pack(layer):
        parts = [
            lax.dynamic_slice_in_dim(w[layer], core * half, half, 1).astype(BF16)
            for w in (query_weight, key_weight, value_weight, output_weight)
        ]
        return jnp.concatenate(parts, axis=1)

    def feed_pack(layer, place):
        rows = inner_weight.shape[1]
        first = inner_weight[layer].reshape(rows, n, 4, quarter)
        first = lax.dynamic_index_in_dim(first, core * 2 + place, 2, keepdims=False)
        second = outer_weight[layer].reshape(4, quarter, width)
        second = lax.dynamic_index_in_dim(second, core * 2 + place, 0, keepdims=False)
        return jnp.concatenate([first.reshape(rows, wide).astype(BF16), second.astype(BF16)], axis=0)

    vectors = [
        query_bias, value_bias, output_bias, first_gain, first_shift,
        outer_bias, second_gain, second_shift, inner_bias,
    ]

    packs = {}
    packs["a0"] = attention_pack(0)
    chunks_a0, dist_long = ring.gather(packs["a0"], True)
    vector_pack = jnp.concatenate([v.astype(BF16) for v in vectors], axis=1)
    gathered_vectors = lax.all_gather(vector_pack, "ctx", axis=0)
    feed0 = tie(feed_pack(0, x), chunks_a0[3])
    chunks_f0, dist_short = ring.gather(feed0, False)
    others_f0 = [x_swap(c) for c in chunks_f0[1:]]
    attn1 = tie(attention_pack(1), chunks_f0[3])
    chunks_a1, _ = ring.gather(attn1, True)
    feed1 = tie(feed_pack(1, x), chunks_a1[3])
    chunks_f1, _ = ring.gather(feed1, False)
    others_f1 = [x_swap(c) for c in chunks_f1[1:]]

    owners_long = jnp.stack([ring.member(d) for d in dist_long]).astype(jnp.int32)
    owners_short = jnp.stack([ring.member(d) for d in dist_short]).astype(jnp.int32)
    places = jnp.stack([x, 1 - x]).astype(jnp.int32)

    def layer_weights(layer, chunks_a, chunks_f, others_f):
        qkv, out_half = assemble_attention(chunks_a, owners_long)
        qkv = qkv.reshape(width, 3 * half)
        out_half = out_half.reshape(width, half)
        mine = lax.dynamic_slice_in_dim(out_half, core * half, half, 0)
        theirs = core_swap(lax.dynamic_slice_in_dim(out_half, (1 - core) * half, half, 0))
        out_rows = ordered(core, mine, theirs, 1)
        first, second = assemble_feed(chunks_f, [feed_pack(layer, 1 - x)] + others_f, owners_short, places)
        return qkv[:, :half], qkv[:, half:], out_rows, first.reshape(width, 2 * wide), second.reshape(2 * wide, width)

    weights = [
        layer_weights(0, chunks_a0, chunks_f0, others_f0),
        layer_weights(1, chunks_a1, chunks_f1, others_f1),
    ]

    per = width // n

    def layer_vectors(layer):
        g = gathered_vectors[:, layer].astype(F32)
        flat = [g[:, i * per : (i + 1) * per].reshape(-1) for i in range(8)]
        inner = g[:, 8 * per :].reshape(n, 2, 2, quarter)
        inner = lax.dynamic_index_in_dim(inner, core, 1, keepdims=False)
        inner = jnp.transpose(inner, (1, 0, 2)).reshape(-1)
        mine = [lax.dynamic_slice_in_dim(v, core * half, half) for v in flat[:2]]
        return mine + flat[2:] + [inner]

    own_ids = segment_ids.reshape(-1)
    ids = [slot_ids(own_ids, tokens, n), slot_ids(core_swap(own_ids), tokens, n)]
    key_ids = jnp.stack(ids)
    query_ids = key_ids[:, OWN]
    low, high = jnp.min(query_ids, axis=1), jnp.max(query_ids, axis=1)
    need = (jnp.max(key_ids, axis=2) >= low[:, None]) & (jnp.min(key_ids, axis=2) <= high[:, None])
    need = need.astype(jnp.int32).reshape(-1)
    query_ids = query_ids.reshape(2, 1, tokens)
    key_ids = key_ids.reshape(2, SLOTS * tokens, 1)

    def both(value):
        return jnp.concatenate([value, core_swap(value)], axis=0)

    def sum_cores(partial):
        return partial[:tokens] + core_swap(partial[tokens:])

    hidden = hidden_in.astype(F32)
    saved = []
    for layer in range(LAYERS):
        wq, wkv, wo, w1, w2 = weights[layer]
        bq, bv, bo, g1, c1, b2, g2, c2, b1 = layer_vectors(layer)
        rounded = hidden.astype(BF16)
        window = widen(rounded, n)
        window = jnp.stack([window, core_swap(window)])
        rows = window[:, OWN].reshape(2 * tokens, width)
        flat = window.reshape(2 * SLOTS * tokens, width)
        queries = ((dot(rows, wq, NN) + bq) * scale).astype(BF16).reshape(2, tokens, half)
        kv_bias = jnp.concatenate([jnp.zeros_like(bv), bv])
        keys_values = (dot(flat, wkv, NN) + kv_bias).astype(BF16).reshape(2, SLOTS, tokens, width)
        mixed, lse = attend(queries, keys_values, query_ids, key_ids, need)
        mixed_rows = mixed.reshape(2 * tokens, half)
        first_sum = hidden + (sum_cores(dot(mixed_rows, wo, NN)) + bo)
        settled = normalize(first_sum, g1, c1)
        settled_rows = both(settled.astype(BF16))
        inner = dot(settled_rows, w1, NN) + b1
        cdf = (1.0 + lax.erf(inner * (0.5**0.5))) * 0.5
        activated = (inner * cdf).astype(BF16)
        slope = cdf + inner * jnp.exp(-0.5 * inner * inner) * (0.5 / jnp.pi) ** 0.5
        second_sum = settled + (sum_cores(dot(activated, w2, NN)) + b2)
        hidden = normalize(second_sum, g2, c2)
        saved.append((flat, rows, queries, keys_values, lse, mixed, first_sum, settled_rows, slope, activated, second_sum))
    output = hidden.astype(BF16)

    grad = cotangent.astype(F32)
    layer_grads = [None] * LAYERS
    vector_grads = [None] * LAYERS
    zeros_half = jnp.zeros((width,), F32)
    for layer in reversed(range(LAYERS)):
        wq, wkv, wo, w1, w2 = weights[layer]
        bq, bv, bo, g1, c1, b2, g2, c2, b1 = layer_vectors(layer)
        flat, rows, queries, keys_values, lse, mixed, first_sum, settled_rows, slope, activated, second_sum = saved[layer]
        grad_second, d_g2, d_c2 = normalize_back(second_sum, g2, grad)
        go = grad_second.astype(BF16)
        go_rows = both(go)
        d_w2 = dot(activated, go_rows, TN, BF16).reshape(2, n, quarter, width)
        d_b2 = column_sums(go)
        gi = (slope * dot(go_rows, w2, NT)).astype(BF16)
        d_w1 = dot(settled_rows, gi, TN, BF16)
        d_b1 = column_sums(gi)
        gset = grad_second + sum_cores(dot(gi, w1, NT))
        grad_first, d_g1, d_c1 = normalize_back(first_sum, g1, gset)
        gb = grad_first.astype(BF16)
        gb_rows = both(gb)
        d_wo = dot(mixed.reshape(2 * tokens, half), gb_rows, TN, BF16)
        d_bo = column_sums(gb)
        gm = dot(gb_rows, wo, NT, BF16).reshape(2, tokens, half)
        gq, gk, gv = attend_back(queries, keys_values, gm, mixed, lse, query_ids, key_ids, need)
        gq = gq.reshape(2 * tokens, half)
        gk = gk.reshape(2 * SLOTS * tokens, half)
        gv = gv.reshape(2 * SLOTS * tokens, half)
        d_bq = column_sums(gq)
        d_bv = column_sums(gv)
        d_wq = dot(rows, gq, TN, BF16)
        d_wk = dot(flat, gk, TN, BF16)
        d_wv = dot(flat, gv, TN, BF16)
        du_rows = dot(gq, wq, NT)
        du = (dot(gk, wkv[:, :half], NT) + dot(gv, wkv[:, half:], NT)).reshape(2, SLOTS, tokens, width)
        du = du.at[:, OWN].add(du_rows.reshape(2, tokens, width))
        du = du.astype(BF16)
        du_own = du[0].astype(F32) + core_swap(du[1]).astype(F32)
        grad = grad_first + give_back(du_own, n)

        def outer_part(t, d_w2=d_w2):
            return lax.dynamic_index_in_dim(d_w2, t, 1, keepdims=False).astype(F32)

        sum_w2 = ring.scatter(outer_part, True).astype(BF16)
        sum_w2 = (sum_w2.astype(F32) + x_swap(sum_w2).astype(F32)).astype(BF16)
        sum_w2 = sum_w2.reshape(2 * quarter, width)
        out_w2 = ordered(core, sum_w2, core_swap(sum_w2), 0).astype(F32)

        give = lax.dynamic_slice_in_dim(d_w1, (1 - x) * wide, wide, 1)
        keep = lax.dynamic_slice_in_dim(d_w1, x * wide, wide, 1).reshape(n, per, wide)
        came = x_swap(give).reshape(n, per, wide)

        def inner_part(t, keep=keep, came=came):
            mine = lax.dynamic_index_in_dim(keep, t, 0, keepdims=False).astype(F32)
            return mine + lax.dynamic_index_in_dim(came, t, 0, keepdims=False).astype(F32)

        sum_w1 = ring.scatter(inner_part, False).astype(BF16)
        pair_w1 = ordered(x, sum_w1.reshape(per, n, 1, quarter), x_swap(sum_w1).reshape(per, n, 1, quarter), 2)
        pair_w1 = pair_w1.reshape(per, n, 1, 2 * quarter)
        out_w1 = ordered(core, pair_w1, core_swap(pair_w1), 2).reshape(per, ff).astype(F32)

        give = lax.dynamic_slice_in_dim(d_wo, (1 - core) * half, half, 1)
        keep = lax.dynamic_slice_in_dim(d_wo, core * half, half, 1)
        d_wo = ordered(core, keep, core_swap(give), 0)
        pieces = [d.reshape(n, per, half) for d in (d_wq, d_wk, d_wv, d_wo)]

        def attention_part(t, pieces=pieces):
            return jnp.concatenate(
                [lax.dynamic_index_in_dim(p, t, 0, keepdims=False) for p in pieces], axis=1
            ).astype(F32)

        sum_a = ring.scatter(attention_part, True).astype(BF16)
        sum_a = (sum_a.astype(F32) + x_swap(sum_a).astype(F32)).astype(BF16)
        peer_a = core_swap(sum_a)
        outs_a = [
            ordered(core, sum_a[:, i * half : (i + 1) * half], peer_a[:, i * half : (i + 1) * half], 1).astype(F32)
            for i in range(4)
        ]
        layer_grads[layer] = outs_a + [out_w1, out_w2]

        spread = [
            lax.dynamic_update_slice_in_dim(zeros_half, v, core * half, 0) for v in (d_bq, d_bv)
        ]
        d_b1 = jnp.transpose(d_b1.reshape(2, n, quarter), (1, 0, 2)).reshape(n, 1, 2 * quarter)
        d_b1 = lax.dynamic_update_slice_in_dim(jnp.zeros((n, 2, 2 * quarter), F32), d_b1, core, 1)
        vector_grads[layer] = jnp.concatenate(
            spread + [d_bo, d_g1, d_c1, d_b2, d_g2, d_c2, d_b1.reshape(-1)]
        )

    sums = lax.psum(jnp.stack(vector_grads), ("dp", "ctx"))
    own_vectors = [
        lax.dynamic_slice_in_dim(sums[:, i * width : (i + 1) * width], ctx * per, per, 1) for i in range(8)
    ]
    own_b1 = lax.dynamic_slice_in_dim(sums[:, 8 * width :], ctx * (ff // n), ff // n, 1)
    d_bq, d_bv, d_bo, d_g1, d_c1, d_b2, d_g2, d_c2 = own_vectors
    dq, dk, dv, do, d1, d2 = [jnp.stack(pair) for pair in zip(*layer_grads)]
    return (
        output,
        grad.astype(BF16),
        dq, d_bq, dk, dv, d_bv, do, d_bo, d_g1, d_c1, d1, own_b1, d2, d_b2, d_g2, d_c2,
    )


def solution(mesh):
    tokens = P(("dp", "ctx"), None)
    matrix = P(None, "ctx", None)
    vector = P(None, "ctx")
    params = (
        matrix, vector, matrix, matrix, vector, matrix, vector, vector,
        vector, matrix, vector, matrix, vector, vector, vector,
    )
    return jax.shard_map(
        local,
        mesh=mesh,
        in_specs=(tokens, P("dp", None, None)) + params + (tokens,),
        out_specs=(tokens, tokens) + params,
        check_vma=False,
    )
```

```python
import jax
import jax.numpy as jnp
from jax import lax
from jax.experimental import pallas as pl
from jax.experimental.pallas import tpu as pltpu
from jax.sharding import PartitionSpec as P

HD = 64
LAYERS = 2
SEQ = 2048
SLOTS = 5
OWN = 2
BF16 = jnp.bfloat16
F32 = jnp.float32
CORE_PAIRS = [(i, i ^ 1) for i in range(4)]
X_PAIRS = [(i, i ^ 2) for i in range(4)]


def dot(left, right, dims, out=F32):
    return lax.dot_general(left, right, (dims, ((), ())), preferred_element_type=F32).astype(out)


NN = ((1,), (0,))
NT = ((1,), (1,))
TN = ((0,), (0,))


def core_swap(value):
    return lax.ppermute(value, "dp", CORE_PAIRS)


def x_swap(value):
    return lax.ppermute(value, "dp", X_PAIRS)


def tie(value, *tokens):
    return lax.optimization_barrier((value,) + tokens)[0]


def ordered(place, mine, peer, axis):
    first = jnp.where(place == 0, mine, peer)
    second = jnp.where(place == 0, peer, mine)
    return jnp.concatenate([first, second], axis=axis)


class Ring:
    def __init__(self, n):
        self.n = n
        self.order = [2 * r if r < n // 2 else 2 * (n - 1 - r) + 1 for r in range(n)]
        self.cw = [(self.order[r], self.order[(r + 1) % n]) for r in range(n)]
        self.ccw = [(b, a) for a, b in self.cw]
        ctx = lax.axis_index("ctx")
        self.place = jnp.where(ctx % 2 == 0, ctx // 2, n - 1 - ctx // 2)

    def member(self, distance):
        r = (self.place + distance) % self.n
        return jnp.where(r < self.n // 2, 2 * r, 2 * (self.n - 1 - r) + 1)

    def send(self, value, sign):
        return lax.ppermute(value, "ctx", self.cw if sign > 0 else self.ccw)

    def steps(self, sign, long_sign):
        return self.n // 2 if sign == long_sign else self.n - 1 - self.n // 2


class Beats:
    def __init__(self):
        self.streams = []

    def start(self, stream):
        self.streams.append([stream, next(stream)])

    def beat(self, *state):
        flights = [s[1] for s in self.streams]
        flights, state = lax.optimization_barrier((flights, state))
        alive = []
        for (stream, _), flight in zip(self.streams, flights):
            try:
                alive.append([stream, stream.send(flight)])
            except StopIteration:
                pass
        self.streams = alive
        return state

    def until(self, ready, *state):
        while not ready():
            state = self.beat(*state)
        return state


def once(sent, sink, beats=1):
    for _ in range(beats - 1):
        yield None
    sink.append((yield sent))


class Gather:
    def __init__(self, ring, pack, long_sign):
        self.ring, self.pack, self.long_sign = ring, pack, long_sign
        self.own = None
        self.got = {}

    def value(self):
        if self.own is None:
            self.own = self.pack()
        return self.own

    def stream(self, sign):
        value = self.value()
        for step in range(1, self.ring.steps(sign, self.long_sign) + 1):
            value = yield self.ring.send(value, sign)
            self.got[-sign * step] = value

    def ready(self):
        return len(self.got) == self.ring.n - 1

    def chunks(self):
        distances = sorted(self.got)
        chunks = [self.own] + [self.got[d] for d in distances]
        owners = [self.ring.member(d) for d in [0] + distances]
        return chunks, jnp.stack(owners).astype(jnp.int32)


def gather_stream(gathers, sign):
    for g in gathers:
        yield from g.stream(sign)


class Scatter:
    def __init__(self, ring, part_of, long_sign):
        self.ring, self.part_of, self.long_sign = ring, part_of, long_sign
        self.got = {}

    def stream(self, sign):
        got = None
        for step in range(self.ring.steps(sign, self.long_sign), 0, -1):
            part = self.part_of(self.ring.member(sign * step))
            if got is not None:
                part = part + got.astype(F32)
            got = yield self.ring.send(part.astype(BF16), sign)
        self.got[sign] = got

    def ready(self):
        return len(self.got) == 2

    def total(self):
        return self.part_of(lax.axis_index("ctx")) + self.got[1].astype(F32) + self.got[-1].astype(F32)


def scatter_stream(queue, sign):
    i = 0
    while True:
        while i == len(queue):
            yield None
        if queue[i] is None:
            return
        yield from queue[i].stream(sign)
        i += 1


def assemble(chunks, owners, pieces):
    n = len(chunks)

    def kernel(owner_ref, *refs):
        ins, outs = refs[:n], refs[n:]
        for i in range(n):
            for (r0, r1, c0, c1), out in zip(pieces, outs):
                out[owner_ref[i]] = ins[i][r0:r1, c0:c1]

    return pl.pallas_call(
        kernel,
        out_shape=tuple(jax.ShapeDtypeStruct((n, r1 - r0, c1 - c0), BF16) for r0, r1, c0, c1 in pieces),
        in_specs=[pl.BlockSpec(memory_space=pltpu.SMEM)] + [pl.BlockSpec(memory_space=pltpu.VMEM)] * n,
        out_specs=tuple(pl.BlockSpec(memory_space=pltpu.VMEM) for _ in pieces),
    )(owners, *chunks)


SLOT_ORDER = (2, 1, 3, 0, 4)


def head_parts(value):
    lane = lax.broadcasted_iota(jnp.int32, value.shape, 1)
    zero = jnp.zeros_like(value)
    return jnp.where(lane < HD, value, zero), jnp.where(lane < HD, zero, value)


def attend(queries, keys_values, query_ids, key_ids, need, seq):
    _, tokens, width = queries.shape
    pairs = width // 128

    def kernel(need_ref, q_ref, k_ref, v_ref, qseg_ref, kseg_ref, mixed_ref, lse_ref, top, total, acc):
        heads = head_parts(q_ref[0])
        qseg = qseg_ref[0]

        def one_slot(slot, first):
            keys = k_ref[0, slot]
            values = v_ref[0, slot]
            mask = kseg_ref[0, slot * tokens : (slot + 1) * tokens] == qseg
            for h in range(2):
                scores = jnp.where(mask, dot(keys, heads[h], NT), -1e30)
                best = jnp.max(scores, axis=0, keepdims=True)
                if not first:
                    old = top[h]
                    best = jnp.maximum(best, old)
                expo = jnp.exp(scores - best)
                sums = jnp.sum(expo, axis=0, keepdims=True)
                part = dot(values, expo.astype(BF16), TN)
                if not first:
                    shrink = jnp.exp(old - best)
                    sums = sums + total[h] * shrink
                    part = part + acc[h] * shrink
                top[h] = best
                total[h] = sums
                acc[h] = part

        one_slot(OWN, True)
        for slot in SLOT_ORDER[1:]:

            @pl.when(need_ref[seq * SLOTS + slot] > 0)
            def _(slot=slot):
                one_slot(slot, False)

        halves = [acc[h][HD * h : HD * (h + 1)] / total[h] for h in range(2)]
        mixed_ref[0] = jnp.concatenate(halves, axis=0).T.astype(BF16)
        lse_ref[0] = jnp.concatenate([top[h] + jnp.log(total[h]) for h in range(2)], axis=0)

    return pl.pallas_call(
        kernel,
        grid_spec=pltpu.PrefetchScalarGridSpec(
            num_scalar_prefetch=1,
            grid=(pairs,),
            in_specs=[
                pl.BlockSpec((1, tokens, 128), lambda p, n: (seq, 0, p)),
                pl.BlockSpec((1, SLOTS, tokens, 128), lambda p, n: (seq, 0, 0, p)),
                pl.BlockSpec((1, SLOTS, tokens, 128), lambda p, n: (seq, 0, 0, pairs + p)),
                pl.BlockSpec((1, 1, tokens), lambda p, n: (seq, 0, 0)),
                pl.BlockSpec((1, SLOTS * tokens, 1), lambda p, n: (seq, 0, 0)),
            ],
            out_specs=[
                pl.BlockSpec((1, tokens, 128), lambda p, n: (0, 0, p)),
                pl.BlockSpec((1, 2, tokens), lambda p, n: (p, 0, 0)),
            ],
            scratch_shapes=[
                pltpu.VMEM((2, 1, tokens), F32),
                pltpu.VMEM((2, 1, tokens), F32),
                pltpu.VMEM((2, 128, tokens), F32),
            ],
        ),
        out_shape=(
            jax.ShapeDtypeStruct((1, tokens, width), BF16),
            jax.ShapeDtypeStruct((pairs, 2, tokens), F32),
        ),
    )(need, queries, keys_values, keys_values, query_ids, key_ids)


def attend_back(queries, keys_values, grad_mixed, lse, query_ids, key_ids, need, seq):
    _, tokens, width = queries.shape
    pairs = width // 128

    def kernel(
        need_ref, q_ref, k_ref, v_ref, g_ref, lse_ref, qseg_ref, kseg_ref,
        gq_ref, gk_ref, gv_ref, probs_ref, grads_ref, inner_ref, acc,
    ):
        heads = head_parts(q_ref[0])
        grads = head_parts(g_ref[0])
        qseg = qseg_ref[0]

        def when(slot, body):
            if slot == OWN:
                body()
            else:
                pl.when(need_ref[seq * SLOTS + slot] > 0)(body)

        def probabilities(slot):
            mask = kseg_ref[0, slot * tokens : (slot + 1) * tokens] == qseg
            for h in range(2):
                scores = jnp.where(mask, dot(k_ref[0, slot], heads[h], NT), -1e30)
                probs = jnp.exp(scores - lse_ref[0, h : h + 1])
                grad_probs = dot(v_ref[0, slot], grads[h], NT)
                part = jnp.sum(probs * grad_probs, axis=0, keepdims=True)
                probs_ref[h, slot] = probs
                grads_ref[h, slot] = grad_probs
                inner_ref[h] = part if slot == OWN else inner_ref[h] + part

        def gradients(slot):
            key_grad = value_grad = None
            for h in range(2):
                probs = probs_ref[h, slot]
                grad_scores = (probs * (grads_ref[h, slot] - inner_ref[h])).astype(BF16)
                part = dot(k_ref[0, slot], grad_scores, TN)
                acc[h] = part if slot == OWN else acc[h] + part
                key_part = dot(grad_scores, heads[h], NN)
                value_part = dot(probs.astype(BF16), grads[h], NN)
                key_grad = key_part if h == 0 else key_grad + key_part
                value_grad = value_part if h == 0 else value_grad + value_part
            gk_ref[0, slot] = key_grad.astype(BF16)
            gv_ref[0, slot] = value_grad.astype(BF16)

        for slot in SLOT_ORDER:
            when(slot, lambda slot=slot: probabilities(slot))
        for slot in SLOT_ORDER:
            when(slot, lambda slot=slot: gradients(slot))
            if slot != OWN:

                @pl.when(need_ref[seq * SLOTS + slot] == 0)
                def _(slot=slot):
                    gk_ref[0, slot] = jnp.zeros((tokens, 128), BF16)
                    gv_ref[0, slot] = jnp.zeros((tokens, 128), BF16)

        joined = jnp.concatenate([acc[h][HD * h : HD * (h + 1)] for h in range(2)], axis=0)
        gq_ref[0] = joined.T.astype(BF16) * (HD**-0.5)

    row_spec = pl.BlockSpec((1, tokens, 128), lambda p, n: (seq, 0, p))
    out_rows = pl.BlockSpec((1, tokens, 128), lambda p, n: (0, 0, p))
    out_slots = pl.BlockSpec((1, SLOTS, tokens, 128), lambda p, n: (0, 0, 0, p))
    return pl.pallas_call(
        kernel,
        grid_spec=pltpu.PrefetchScalarGridSpec(
            num_scalar_prefetch=1,
            grid=(pairs,),
            in_specs=[
                row_spec,
                pl.BlockSpec((1, SLOTS, tokens, 128), lambda p, n: (seq, 0, 0, p)),
                pl.BlockSpec((1, SLOTS, tokens, 128), lambda p, n: (seq, 0, 0, pairs + p)),
                row_spec,
                pl.BlockSpec((1, 2, tokens), lambda p, n: (p, 0, 0)),
                pl.BlockSpec((1, 1, tokens), lambda p, n: (seq, 0, 0)),
                pl.BlockSpec((1, SLOTS * tokens, 1), lambda p, n: (seq, 0, 0)),
            ],
            out_specs=[out_rows, out_slots, out_slots],
            scratch_shapes=[
                pltpu.VMEM((2, SLOTS, tokens, tokens), F32),
                pltpu.VMEM((2, SLOTS, tokens, tokens), F32),
                pltpu.VMEM((2, 1, tokens), F32),
                pltpu.VMEM((2, 128, tokens), F32),
            ],
        ),
        out_shape=(
            jax.ShapeDtypeStruct((1, tokens, width), BF16),
            jax.ShapeDtypeStruct((1, SLOTS, tokens, width), BF16),
            jax.ShapeDtypeStruct((1, SLOTS, tokens, width), BF16),
        ),
    )(need, queries, keys_values, keys_values, grad_mixed, lse, query_ids, key_ids)


def normalize(operand, gain, shift):
    centered = operand - jnp.mean(operand, axis=-1, keepdims=True)
    spread = jnp.mean(centered * centered, axis=-1, keepdims=True)
    return centered * lax.rsqrt(spread + 1e-05) * gain + shift


def normalize_back(operand, gain, grad):
    centered = operand - jnp.mean(operand, axis=-1, keepdims=True)
    spread = jnp.mean(centered * centered, axis=-1, keepdims=True)
    inverse = lax.rsqrt(spread + 1e-05)
    unit = centered * inverse
    scaled = grad * gain
    out = inverse * (
        scaled
        - jnp.mean(scaled, axis=-1, keepdims=True)
        - unit * jnp.mean(scaled * unit, axis=-1, keepdims=True)
    )
    return out, jnp.sum(grad * unit, axis=0), jnp.sum(grad, axis=0)


def column_sums(operand):
    return jnp.sum(operand.astype(F32), axis=0)


def shifts(n, by):
    return [(i, i + by) for i in range(n) if 0 <= i + by < n]


def slot_ids(group_ids, tokens, n):
    ctx = lax.axis_index("ctx")
    per = SEQ // tokens
    odd = ctx % 2 == 1
    blocks = [ctx - 2, ctx ^ 1, ctx, jnp.where(odd, ctx + 1, ctx - 1), ctx + 2]
    out = []
    for block in blocks:
        inside = (block >= 0) & (block < n) & (block // per == ctx // per)
        start = jnp.clip(block, 0, n - 1) * tokens
        out.append(jnp.where(inside, lax.dynamic_slice_in_dim(group_ids, start, tokens), -1))
    return jnp.stack(out)


def local(
    hidden_in,
    segment_ids,
    query_weight,
    query_bias,
    key_weight,
    value_weight,
    value_bias,
    output_weight,
    output_bias,
    first_gain,
    first_shift,
    inner_weight,
    inner_bias,
    outer_weight,
    outer_bias,
    second_gain,
    second_shift,
    cotangent,
):
    tokens, width = hidden_in.shape
    n = lax.axis_size("ctx")
    ctx = lax.axis_index("ctx")
    dp = lax.axis_index("dp")
    core = dp % 2
    x = dp // 2
    half = width // 2
    ff = inner_weight.shape[2]
    per = width // n
    quarter = ff // (4 * n)
    wide = ff // 4
    scale = HD**-0.5
    ring = Ring(n)
    beats = Beats()
    odd = ctx % 2 == 1
    beside_pairs = [(i, i ^ 1) for i in range(n)]

    vectors = [
        query_bias, value_bias, output_bias, first_gain, first_shift,
        outer_bias, second_gain, second_shift, inner_bias,
    ]
    vector_size = LAYERS * (8 * per + ff // n)
    vector_rows = -(-vector_size // (4 * half * 16)) * 16

    def attention_pack(layer):
        parts = [
            lax.dynamic_slice_in_dim(w[layer], core * half, half, 1).astype(BF16)
            for w in (query_weight, key_weight, value_weight, output_weight)
        ]
        pack = jnp.concatenate(parts, axis=1)
        if layer == 0:
            flat = jnp.concatenate([v.astype(BF16) for v in vectors], axis=1).reshape(-1)
            flat = jnp.pad(flat, (0, vector_rows * 4 * half - vector_size))
            pack = jnp.concatenate([pack, flat.reshape(vector_rows, 4 * half)], axis=0)
        return pack

    def inner_pack(layer):
        block = inner_weight[layer].reshape(per, n, 4, quarter)
        block = lax.dynamic_index_in_dim(block, core * 2 + x, 2, keepdims=False)
        return block.astype(BF16).reshape(per, wide)

    def outer_pack(layer, place):
        block = outer_weight[layer].reshape(4, quarter, width)
        return lax.dynamic_index_in_dim(block, core * 2 + place, 0, keepdims=False).astype(BF16)

    attn = [Gather(ring, lambda l=l: attention_pack(l), 1) for l in range(LAYERS)]
    inner_w = [Gather(ring, lambda l=l: inner_pack(l), -1) for l in range(LAYERS)]
    outer_w = [
        Gather(ring, lambda: outer_pack(0, x), 1),
        Gather(ring, lambda: jnp.concatenate([outer_pack(1, x), outer_pack(1, 1 - x)], axis=0), -1),
    ]
    order = [attn[0], inner_w[0], outer_w[0], inner_w[1], attn[1], outer_w[1]]
    beats.start(gather_stream(order, 1))
    beats.start(gather_stream(order, -1))

    swapped = {}

    def pass_on(gather, name, parts):
        chunks, owners = gather.chunks()
        (whole,) = assemble(chunks, owners, [(0, per if name[0] == "i" else quarter, 0, width)])
        whole = whole.reshape(-1, width)
        swapped[name] = [whole, []]
        rows = whole.shape[0] // parts
        for i in range(parts):
            beats.start(later(whole[i * rows : (i + 1) * rows], swapped[name][1], i))

    def later(value, sink, wait):
        for _ in range(wait):
            yield None
        sink.append((yield x_swap(value)))

    def has(name, parts):
        return name in swapped and len(swapped[name][1]) == parts

    def watch(*state):
        state = beats.beat(*state)
        for gather, name in ((inner_w[0], "i0"), (outer_w[0], "o0"), (inner_w[1], "i1")):
            if gather.ready() and name not in swapped:
                pass_on(gather, name, 4)
        return state

    def watch_until(ready, *state):
        while not ready():
            state = watch(*state)
        return state

    own_ids = segment_ids.reshape(-1)
    key_ids = jnp.stack([slot_ids(own_ids, tokens, n), slot_ids(core_swap(own_ids), tokens, n)])
    query_ids = key_ids[:, OWN]
    low, high = jnp.min(query_ids, axis=1), jnp.max(query_ids, axis=1)
    need = (jnp.max(key_ids, axis=2) >= low[:, None]) & (jnp.min(key_ids, axis=2) <= high[:, None])
    need = need.astype(jnp.int32).reshape(-1)
    query_ids = query_ids.reshape(2, 1, tokens)
    key_ids = key_ids.reshape(2, SLOTS * tokens, 1)

    def both(value):
        return jnp.concatenate([value, core_swap(value)], axis=0)

    def sum_cores(partial):
        return partial[:tokens] + core_swap(partial[tokens:])

    def window_streams(own, sink):
        def ends():
            behind = yield lax.ppermute(own, "ctx", shifts(n, 2))
            sink["behind"] = behind

        def front():
            ahead = yield lax.ppermute(own, "ctx", shifts(n, -2))
            sink["ahead"] = ahead

        def side():
            beside = yield lax.ppermute(own, "ctx", beside_pairs)
            sink["beside"] = beside
            send = jnp.where(odd, sink["behind"], sink["ahead"])
            sink["across"] = yield lax.ppermute(send, "ctx", beside_pairs)

        for stream in (ends(), front(), side()):
            beats.start(stream)

    def window_of(own, sink):
        blocks = [sink["behind"], sink["beside"], own, sink["across"], sink["ahead"]]
        mine = jnp.stack(blocks)
        return jnp.stack([mine, core_swap(mine)])

    hidden = hidden_in.astype(F32)
    rounded = hidden_in
    sink = {}
    window_streams(rounded, sink)
    saved = []
    gathered_vectors = None
    weights = []
    for layer in range(LAYERS):
        hidden, rounded = watch_until(
            lambda layer=layer, sink=sink: attn[layer].ready() and "across" in sink, hidden, rounded
        )
        window = window_of(rounded, sink)
        chunks, owners = attn[layer].chunks()
        pieces = [(0, per, 0, 3 * half), (0, per, 3 * half, 4 * half)]
        if layer == 0:
            pieces.append((per, per + vector_rows, 0, 4 * half))
            qkv, out_half, vector_block = assemble(chunks, owners, pieces)
            gathered_vectors = vector_block.reshape(n, -1)[:, :vector_size].reshape(n, LAYERS, -1)
        else:
            qkv, out_half = assemble(chunks, owners, pieces)
        qkv = qkv.reshape(width, 3 * half)
        out_half = out_half.reshape(width, half)
        theirs = core_swap(lax.dynamic_slice_in_dim(out_half, (1 - core) * half, half, 0))
        wo = ordered(core, lax.dynamic_slice_in_dim(out_half, core * half, half, 0), theirs, 1)
        wq, wkv = qkv[:, :half], qkv[:, half:]

        block = gathered_vectors[:, layer].astype(F32)
        flat_vectors = [block[:, i * per : (i + 1) * per].reshape(-1) for i in range(8)]
        b1 = lax.dynamic_index_in_dim(block[:, 8 * per :].reshape(n, 2, 2, quarter), core, 1, keepdims=False)
        b1_mine = lax.dynamic_index_in_dim(b1, x, 1, keepdims=False).reshape(-1)
        b1_other = lax.dynamic_index_in_dim(b1, 1 - x, 1, keepdims=False).reshape(-1)
        bq, bv = [lax.dynamic_slice_in_dim(v, core * half, half) for v in flat_vectors[:2]]
        bo, g1, c1, b2, g2, c2 = flat_vectors[2:]

        rows = window[:, OWN].reshape(2 * tokens, width)
        flat = window.reshape(2 * SLOTS * tokens, width)
        queries = ((dot(rows, wq, NN) + bq) * scale).astype(BF16).reshape(2, tokens, half)
        kv_bias = jnp.concatenate([jnp.zeros_like(bv), bv])
        keys_values = (dot(flat, wkv, NN) + kv_bias).astype(BF16).reshape(2, SLOTS, tokens, width)
        hidden, queries, keys_values = watch(hidden, queries, keys_values)
        mixed0, lse0 = attend(queries, keys_values, query_ids, key_ids, need, 0)
        hidden, mixed0, queries, keys_values = watch(hidden, mixed0, queries, keys_values)
        mixed1, lse1 = attend(queries, keys_values, query_ids, key_ids, need, 1)
        hidden, mixed0, mixed1 = watch(hidden, mixed0, mixed1)
        mixed = jnp.concatenate([mixed0, mixed1], axis=0).reshape(2 * tokens, half)
        first_sum = hidden + (sum_cores(dot(mixed, wo, NN)) + bo)
        settled = normalize(first_sum, g1, c1)
        settled_rows = both(settled.astype(BF16))
        name = str(layer)
        settled, settled_rows = watch_until(lambda: has("i" + name, 4), settled, settled_rows)
        w1_mine, w1_other = swapped["i" + name][0], jnp.concatenate(swapped["i" + name][1], axis=0)

        def feed(weight, bias, settled_rows=settled_rows):
            inner = dot(settled_rows, weight, NN) + bias
            cdf = (1.0 + lax.erf(inner * (0.5**0.5))) * 0.5
            slope = cdf + inner * jnp.exp(-0.5 * inner * inner) * (0.5 / jnp.pi) ** 0.5
            return (inner * cdf).astype(BF16), slope

        act_mine, slope_mine = feed(w1_mine, b1_mine)
        act_other, slope_other = feed(w1_other, b1_other)
        if layer == 0:
            settled, act_mine, act_other = watch_until(lambda: has("o0", 4), settled, act_mine, act_other)
            w2_mine, w2_other = swapped["o0"][0], jnp.concatenate(swapped["o0"][1], axis=0)
        else:
            settled, act_mine, act_other = watch_until(outer_w[1].ready, settled, act_mine, act_other)
            chunks, owners = outer_w[1].chunks()
            w2_mine, w2_other = assemble(
                chunks, owners, [(0, quarter, 0, width), (quarter, 2 * quarter, 0, width)]
            )
            w2_mine, w2_other = w2_mine.reshape(-1, width), w2_other.reshape(-1, width)
        outer = dot(act_mine, w2_mine, NN) + dot(act_other, w2_other, NN)
        second_sum = settled + (sum_cores(outer) + b2)
        hidden = normalize(second_sum, g2, c2)
        weights.append((wq, wkv, wo, w1_mine, w1_other, w2_mine, w2_other, g1, g2))
        saved.append(
            (
                flat, rows, queries, keys_values, lse0, lse1, mixed, first_sum, settled_rows,
                slope_mine, slope_other, act_mine, act_other, second_sum,
            )
        )
        if layer + 1 < LAYERS:
            rounded = hidden.astype(BF16)
            sink = {}
            window_streams(rounded, sink)
    output = hidden.astype(BF16)

    queue = []
    beats.start(scatter_stream(queue, 1))
    beats.start(scatter_stream(queue, -1))
    finished = []

    def owned(grad, joined):
        low_sum = grad.astype(BF16)
        return low_sum.astype(F32) + joined(x_swap(low_sum)).astype(F32)

    def turn(value):
        return jnp.concatenate([value[quarter:], value[:quarter]], axis=0)

    jobs = []

    def settle():
        for job in list(jobs):
            if job[0].ready():
                job[1](job[0].total())
                jobs.remove(job)

    def step(*state):
        state = beats.beat(*state)
        settle()
        return state

    outputs = [dict() for _ in range(LAYERS)]
    vector_grads = [None] * LAYERS
    grad = cotangent.astype(F32)
    for layer in reversed(range(LAYERS)):
        wq, wkv, wo, w1_mine, w1_other, w2_mine, w2_other, g1, g2 = weights[layer]
        (
            flat, rows, queries, keys_values, lse0, lse1, mixed, first_sum, settled_rows,
            slope_mine, slope_other, act_mine, act_other, second_sum,
        ) = saved[layer]
        out = outputs[layer]
        grad_second, d_g2, d_c2 = normalize_back(second_sum, g2, grad)
        go = grad_second.astype(BF16)
        go_rows = both(go)
        d_b2 = column_sums(go)
        dw2_mine = dot(act_mine, go_rows, TN, BF16).reshape(n, quarter, width)
        dw2_other = dot(act_other, go_rows, TN, BF16).reshape(n, quarter, width)

        def outer_part(t, parts=(dw2_mine, dw2_other)):
            return jnp.concatenate(
                [lax.dynamic_index_in_dim(p, t, 0, keepdims=False) for p in parts], axis=0
            ).astype(F32)

        def outer_done(total, out=out):
            low_sum = total.astype(BF16)

            def finish():
                came = yield x_swap(low_sum)
                whole = low_sum.astype(F32) + turn(came).astype(F32)
                whole = jnp.where(x == 0, whole, turn(whole))
                out["outer"] = ordered(core, whole, core_swap(whole), 0)

            beats.start(finish())

        queue.append(Scatter(ring, outer_part, 1))
        jobs.append((queue[-1], outer_done))
        grad_second, go_rows = step(grad_second, go_rows)
        gi_other = (slope_other * dot(go_rows, w2_other, NT)).astype(BF16)
        give = dot(settled_rows, gi_other, TN, BF16)
        gi_mine = (slope_mine * dot(go_rows, w2_mine, NT)).astype(BF16)
        came = []
        for i in range(4):
            rows_i = width // 4
            beats.start(later(give[i * rows_i : (i + 1) * rows_i], came, i))
        grad_second, gi_mine, gi_other = step(grad_second, gi_mine, gi_other)
        keep = dot(settled_rows, gi_mine, TN, BF16).reshape(n, per, wide)
        d_b1 = [column_sums(g).reshape(n, 1, 1, quarter) for g in (gi_mine, gi_other)]
        gset = grad_second + sum_cores(dot(gi_mine, w1_mine, NT) + dot(gi_other, w1_other, NT))
        grad_first, d_g1, d_c1 = normalize_back(first_sum, g1, gset)
        gb = grad_first.astype(BF16)
        gb_rows = both(gb)
        d_bo = column_sums(gb)
        grad_first, gb_rows, keep = step(grad_first, gb_rows, keep)
        d_wo = dot(mixed, gb_rows, TN, BF16)
        gm = dot(gb_rows, wo, NT, BF16).reshape(2, tokens, half)
        give = lax.dynamic_slice_in_dim(d_wo, (1 - core) * half, half, 1)
        d_wo = ordered(core, lax.dynamic_slice_in_dim(d_wo, core * half, half, 1), core_swap(give), 0)
        grad_first, gm, d_wo = step(grad_first, gm, d_wo)
        gq0, gk0, gv0 = attend_back(queries, keys_values, gm, lse0, query_ids, key_ids, need, 0)
        grad_first, gm, gq0, gk0, gv0 = step(grad_first, gm, gq0, gk0, gv0)

        def inner_part(t, keep=keep, came=came):
            other = jnp.concatenate(came, axis=0).reshape(n, per, wide)
            mine = lax.dynamic_index_in_dim(keep, t, 0, keepdims=False).astype(F32)
            return mine + lax.dynamic_index_in_dim(other, t, 0, keepdims=False).astype(F32)

        def inner_done(total, out=out):
            low_sum = total.astype(BF16)

            def finish():
                came = yield x_swap(low_sum)
                pair = ordered(x, low_sum.reshape(per, n, 1, quarter), came.reshape(per, n, 1, quarter), 2)
                pair = pair.reshape(per, n, 1, 2 * quarter)
                out["inner"] = ordered(core, pair, core_swap(pair), 2).reshape(per, ff).astype(F32)

            beats.start(finish())

        gq1, gk1, gv1 = attend_back(queries, keys_values, gm, lse1, query_ids, key_ids, need, 1)
        while len(came) < 4:
            grad_first, gq0, gk0, gv0, gq1, gk1, gv1 = step(grad_first, gq0, gk0, gv0, gq1, gk1, gv1)
        queue.append(Scatter(ring, inner_part, -1))
        jobs.append((queue[-1], inner_done))

        gq = jnp.concatenate([gq0, gq1], axis=0).reshape(2 * tokens, half)
        gk = jnp.concatenate([gk0, gk1], axis=0).reshape(2 * SLOTS * tokens, half)
        gv = jnp.concatenate([gv0, gv1], axis=0).reshape(2 * SLOTS * tokens, half)
        pieces = [d.reshape(n, per, half) for d in (
            dot(rows, gq, TN, BF16), dot(flat, gk, TN, BF16), dot(flat, gv, TN, BF16), d_wo)]

        def spread(value):
            return lax.dynamic_update_slice_in_dim(jnp.zeros((width,), F32), value, core * half, 0)

        d_bq, d_bv = spread(column_sums(gq)), spread(column_sums(gv))
        b1_grad = ordered(x, d_b1[0], d_b1[1], 2).reshape(n, 1, 2 * quarter)
        b1_grad = lax.dynamic_update_slice_in_dim(jnp.zeros((n, 2, 2 * quarter), F32), b1_grad, core, 1)
        vector_grads[layer] = jnp.concatenate(
            [v.reshape(n, per) for v in (d_bq, d_bv, d_bo, d_g1, d_c1, d_b2, d_g2, d_c2)]
            + [b1_grad.reshape(n, ff // n)],
            axis=1,
        )
        if layer == 0:
            tail = jnp.concatenate(vector_grads, axis=1)
            tail = jnp.pad(tail, ((0, 0), (0, vector_rows * 4 * half - vector_size)))
            tail = tail.reshape(n, vector_rows, 4 * half)

        def attention_part(t, pieces=pieces, layer=layer):
            part = jnp.concatenate(
                [lax.dynamic_index_in_dim(p, t, 0, keepdims=False) for p in pieces], axis=1
            ).astype(F32)
            if layer == 0:
                part = jnp.concatenate([part, lax.dynamic_index_in_dim(tail, t, 0, keepdims=False)], axis=0)
            return part

        def attention_done(total, out=out, layer=layer):
            low_sum = total.astype(BF16)

            def finish():
                came = yield x_swap(low_sum)
                whole = low_sum.astype(F32) + came.astype(F32)
                peer = core_swap(whole)
                out["attn"] = [
                    ordered(core, whole[:per, i * half : (i + 1) * half], peer[:per, i * half : (i + 1) * half], 1)
                    for i in range(4)
                ]
                if layer == 0:
                    out["vectors"] = (whole[per:] + peer[per:]).reshape(-1)[:vector_size].reshape(LAYERS, -1)

            beats.start(finish())

        queue.append(Scatter(ring, attention_part, 1))
        jobs.append((queue[-1], attention_done))
        grad_first, gq, gk, gv = step(grad_first, gq, gk, gv)
        du_rows = dot(gq, wq, NT)
        du = (dot(gk, wkv[:, :half], NT) + dot(gv, wkv[:, half:], NT)).reshape(2, SLOTS, tokens, width)
        du = du.at[:, OWN].add(du_rows.reshape(2, tokens, width)).astype(BF16)
        parts = du[0].astype(F32) + core_swap(du[1]).astype(F32)
        grad_first, parts = step(grad_first, parts)
        back = {}

        def send(name, value, pairs):
            def stream():
                back[name] = (yield lax.ppermute(value.astype(BF16), "ctx", pairs)).astype(F32)

            beats.start(stream())

        send("across", parts[3], beside_pairs)
        send("beside", parts[1], beside_pairs)
        (own_part,) = step(grad_first + parts[2])
        behind = parts[0] + jnp.where(odd, back["across"], 0.0)
        ahead = parts[4] + jnp.where(odd, 0.0, back["across"])
        send("ahead", behind, shifts(n, -2))
        send("behind", ahead, shifts(n, 2))
        (own_part,) = step(own_part + back["beside"])
        grad = own_part + back["ahead"] + back["behind"]
    queue.append(None)
    while beats.streams or jobs:
        step()

    fields = outputs[0]["vectors"]
    own_vectors = [fields[:, i * per : (i + 1) * per] for i in range(8)] + [fields[:, 8 * per :]]
    d_bq, d_bv, d_bo, d_g1, d_c1, d_b2, d_g2, d_c2, d_b1 = own_vectors
    dq, dk, dv, do = [jnp.stack([o["attn"][i] for o in outputs]) for i in range(4)]
    d1 = jnp.stack([o["inner"] for o in outputs])
    d2 = jnp.stack([o["outer"] for o in outputs])
    return (
        output,
        grad.astype(BF16),
        dq, d_bq, dk, dv, d_bv, do, d_bo, d_g1, d_c1, d1, d_b1, d2, d_b2, d_g2, d_c2,
    )


def solution(mesh):
    tokens = P(("dp", "ctx"), None)
    matrix = P(None, "ctx", None)
    vector = P(None, "ctx")
    params = (
        matrix, vector, matrix, matrix, vector, matrix, vector, vector,
        vector, matrix, vector, matrix, vector, vector, vector,
    )
    return jax.shard_map(
        local,
        mesh=mesh,
        in_specs=(tokens, P("dp", None, None)) + params + (tokens,),
        out_specs=(tokens, tokens) + params,
        check_vma=False,
    )
```

```python
import jax
import jax.numpy as jnp
from jax import lax
from jax.experimental import pallas as pl
from jax.experimental.pallas import tpu as pltpu
from jax.sharding import PartitionSpec as P

HD = 64
LAYERS = 2
SEQ = 2048
SLOTS = 5
OWN = 2
BF16 = jnp.bfloat16
F32 = jnp.float32
CORE_PAIRS = [(i, i ^ 1) for i in range(4)]
X_PAIRS = [(i, i ^ 2) for i in range(4)]


def dot(left, right, dims, out=F32):
    return lax.dot_general(left, right, (dims, ((), ())), preferred_element_type=F32).astype(out)


NN = ((1,), (0,))
NT = ((1,), (1,))
TN = ((0,), (0,))


def core_swap(value):
    return lax.ppermute(value, "dp", CORE_PAIRS)


def x_swap(value):
    return lax.ppermute(value, "dp", X_PAIRS)


def tie(value, *tokens):
    return lax.optimization_barrier((value,) + tokens)[0]


def ordered(place, mine, peer, axis):
    first = jnp.where(place == 0, mine, peer)
    second = jnp.where(place == 0, peer, mine)
    return jnp.concatenate([first, second], axis=axis)


class Ring:
    def __init__(self, n):
        self.n = n
        self.order = [2 * r if r < n // 2 else 2 * (n - 1 - r) + 1 for r in range(n)]
        self.cw = [(self.order[r], self.order[(r + 1) % n]) for r in range(n)]
        self.ccw = [(b, a) for a, b in self.cw]
        ctx = lax.axis_index("ctx")
        self.place = jnp.where(ctx % 2 == 0, ctx // 2, n - 1 - ctx // 2)

    def member(self, distance):
        r = (self.place + distance) % self.n
        return jnp.where(r < self.n // 2, 2 * r, 2 * (self.n - 1 - r) + 1)

    def send(self, value, sign):
        return lax.ppermute(value, "ctx", self.cw if sign > 0 else self.ccw)

    def steps(self, sign, long_sign):
        return self.n // 2 if sign == long_sign else self.n - 1 - self.n // 2


class Hold:
    def __init__(self, value, beats):
        self.value, self.beats = value, beats


class Beats:
    def __init__(self):
        self.streams = []
        self.kept = []

    def start(self, stream):
        self.streams.append([stream, self.flight(next(stream))])

    def flight(self, sent):
        return sent if isinstance(sent, Hold) else Hold(sent, 1)

    def keep(self, place, name):
        self.kept.append((place, name))

    def beat(self, *state):
        for _, flight in self.streams:
            flight.beats -= 1
        if self.streams and not self.kept and not state and all(f.beats > 0 for _, f in self.streams):
            least = min(f.beats for _, f in self.streams)
            for _, flight in self.streams:
                flight.beats -= least
        due = [s for s in self.streams if s[1].beats == 0]
        kept, self.kept = self.kept, []
        values = ([s[1].value for s in due], [place[name] for place, name in kept], state)
        flights, places, state = lax.optimization_barrier(values)
        for (place, name), value in zip(kept, places):
            place[name] = value
        for entry, flight in zip(due, flights):
            try:
                entry[1] = self.flight(entry[0].send(flight))
            except StopIteration:
                self.streams.remove(entry)
        return state

    def until(self, ready, *state):
        while not ready():
            state = self.beat(*state)
        return state


class Gather:
    def __init__(self, ring, pack, long_sign):
        self.ring, self.pack, self.long_sign = ring, pack, long_sign
        self.own = None
        self.got = {}

    def value(self):
        if self.own is None:
            self.own = self.pack()
        return self.own

    def stream(self, sign):
        value = self.value()
        for step in range(1, self.ring.steps(sign, self.long_sign) + 1):
            value = yield self.ring.send(value, sign)
            self.got[-sign * step] = value

    def ready(self):
        return len(self.got) == self.ring.n - 1

    def chunks(self):
        distances = sorted(self.got)
        chunks = [self.own] + [self.got[d] for d in distances]
        owners = [self.ring.member(d) for d in [0] + distances]
        return chunks, jnp.stack(owners).astype(jnp.int32)


def gather_stream(gathers, sign):
    for g in gathers:
        yield from g.stream(sign)


class Scatter:
    def __init__(self, ring, part_of, long_sign):
        self.ring, self.part_of, self.long_sign = ring, part_of, long_sign
        self.got = {}

    def stream(self, sign):
        got = None
        for step in range(self.ring.steps(sign, self.long_sign), 0, -1):
            part = self.part_of(self.ring.member(sign * step))
            if got is not None:
                part = part + got.astype(F32)
            got = yield self.ring.send(part.astype(BF16), sign)
        self.got[sign] = got

    def ready(self):
        return len(self.got) == 2

    def total(self):
        return self.part_of(lax.axis_index("ctx")) + self.got[1].astype(F32) + self.got[-1].astype(F32)


def busy(us):
    return pl.CostEstimate(flops=int(us * 1.1e9), bytes_accessed=int(us * 3e6), transcendentals=0)


def whole(space=pltpu.VMEM):
    return pl.BlockSpec(memory_space=space)


def pack_layer(weights, inner_weight, outer_weight, layer, core, x, extra):
    query, key, value, out = weights
    _, per, width = query.shape
    half = width // 2
    ff = inner_weight.shape[2]
    n = ff // outer_weight.shape[1]
    quarter = ff // (4 * n)
    more = 0 if extra is None else extra.shape[0]
    picks = [core * 2 + x]

    def kernel(sel_ref, q_ref, k_ref, v_ref, o_ref, *refs):
        pack_ref = refs[-1]
        for p in range(half // 128):
            cols = slice(128 * p, 128 * p + 128)
            pack_ref[:per, 256 * p : 256 * p + 128] = k_ref[0, :, cols].astype(BF16)
            pack_ref[:per, 256 * p + 128 : 256 * p + 256] = v_ref[0, :, cols].astype(BF16)
        pack_ref[:per, 2 * half : 3 * half] = q_ref[0].astype(BF16)
        pack_ref[:per, 3 * half :] = o_ref[0].astype(BF16)
        if more:
            pack_ref[per:] = refs[0][...]

    attention = pl.pallas_call(
        kernel,
        cost_estimate=busy(2),
        grid_spec=pltpu.PrefetchScalarGridSpec(
            num_scalar_prefetch=1,
            grid=(1,),
            in_specs=[pl.BlockSpec((1, per, half), lambda i, c: (layer, 0, c[0]))] * 4 + [whole()] * (more > 0),
            out_specs=pl.BlockSpec((per + more, 4 * half), lambda i, c: (0, 0)),
        ),
        out_shape=jax.ShapeDtypeStruct((per + more, 4 * half), BF16),
    )(core.reshape(1).astype(jnp.int32), query, key, value, out, *([extra] if more else []))

    if quarter % 128:
        feeds = []
        for pick in picks:
            first = inner_weight[layer].reshape(per, n, 4, quarter)
            first = lax.dynamic_index_in_dim(first, pick, 2, keepdims=False).reshape(per, width)
            second = outer_weight[layer].reshape(4, quarter, width)
            second = lax.dynamic_index_in_dim(second, pick, 0, keepdims=False)
            feeds.append(jnp.concatenate([first, second], axis=1).astype(BF16))
        return attention, *feeds

    def feed_kernel(sel_ref, *refs):
        for i, dest in enumerate(refs[-1:]):
            for j in range(n):
                dest[:, j * quarter : (j + 1) * quarter] = refs[i * (n + 1) + j][0].astype(BF16)
            dest[:, width:] = refs[i * (n + 1) + n][0].astype(BF16)

    blocks, args = [], []
    for i in range(1):
        for j in range(n):
            blocks.append(pl.BlockSpec((1, per, quarter), lambda _, c, i=i, j=j: (layer, 0, 4 * j + c[i])))
            args.append(inner_weight)
        blocks.append(pl.BlockSpec((1, quarter, width), lambda _, c, i=i: (layer, c[i], 0)))
        args.append(outer_weight)
    feeds = pl.pallas_call(
        feed_kernel,
        cost_estimate=busy(3),
        grid_spec=pltpu.PrefetchScalarGridSpec(
            num_scalar_prefetch=1,
            grid=(1,),
            in_specs=blocks,
            out_specs=[pl.BlockSpec((per, 4 * half), lambda i, c: (0, 0))],
        ),
        out_shape=[jax.ShapeDtypeStruct((per, 4 * half), BF16)],
    )(jnp.stack(picks).astype(jnp.int32), *args)
    return attention, *feeds


def vector_rows(vectors):
    rows = 16
    total = sum(v.shape[1] for v in vectors)
    if any(v.shape[1] % 128 for v in vectors):
        flat = jnp.concatenate([v.astype(BF16) for v in vectors], axis=1)
        return jnp.pad(flat, ((0, rows - LAYERS), (0, 2048 - total)))

    def kernel(*refs):
        out = refs[-1]
        row = lax.broadcasted_iota(jnp.int32, (rows, 1), 0)
        at = 0
        for ref in refs[:-1]:
            k = ref.shape[1]
            value = jnp.zeros((rows, k), F32)
            for l in range(LAYERS):
                value = jnp.where(row == l, ref[l : l + 1, :], value)
            out[:, at : at + k] = value.astype(BF16)
            at += k
        if at < 2048:
            out[:, at:] = jnp.zeros((rows, 2048 - at), BF16)

    return pl.pallas_call(
        kernel,
        cost_estimate=busy(1),
        in_specs=[whole()] * len(vectors),
        out_specs=whole(),
        out_shape=jax.ShapeDtypeStruct((rows, 2048), BF16),
    )(*vectors)


def assemble(chunks, owners, pieces):
    n = len(chunks)
    wide = chunks[0].shape[1]
    kinds = sorted(set((rows, at) for rows, at, _, _ in pieces))

    def kernel(owner_ref, *refs):
        ins, outs = refs[: n * len(kinds)], refs[n * len(kinds) :]
        for i in range(n):
            for (rows, at, first, size), out in zip(pieces, outs):
                out[owner_ref[i]] = ins[n * kinds.index((rows, at)) + i][:, first : first + size]

    blocks = [pl.BlockSpec((rows, wide), lambda _, o, at=at: (at, 0)) for rows, at in kinds for _ in range(n)]
    return pl.pallas_call(
        kernel,
        cost_estimate=busy(5),
        grid_spec=pltpu.PrefetchScalarGridSpec(
            num_scalar_prefetch=1, grid=(1,), in_specs=blocks, out_specs=[whole() for _ in pieces]
        ),
        out_shape=tuple(jax.ShapeDtypeStruct((n, rows, size), BF16) for rows, _, _, size in pieces),
    )(owners, *(chunks * len(kinds)))


SLOT_ORDER = (2, 1, 3, 0, 4)


def two_heads(value):
    lane = lax.broadcasted_iota(jnp.int32, value.shape, 1)
    zero = jnp.zeros_like(value)
    return jnp.concatenate([jnp.where(lane < HD, value, zero), jnp.where(lane < HD, zero, value)], axis=0)


def own_lanes(value, tokens):
    return jnp.concatenate([value[:HD, :tokens], value[HD:, tokens:]], axis=0).T


def attend(window, weights, query_bias, value_bias, query_ids, key_ids, need, seq):
    tokens, width = window[0].shape
    half = width // 2
    pairs = half // 128

    def kernel(need_ref, *refs):
        u = refs[:SLOTS]
        (wkv_ref, wq_ref, bq_ref, bv_ref, qseg_ref, kseg_ref, q_ref, kv_ref, mixed_ref, lse_ref, top, total, acc) = refs[SLOTS:]
        value_lane = lax.broadcasted_iota(jnp.int32, (1, 256), 1) >= 128
        bias = jnp.where(value_lane, jnp.concatenate([bv_ref[...], bv_ref[...]], axis=1), 0.0)
        q = ((dot(u[OWN][...], wq_ref[...], NN) + bq_ref[...]) * (HD**-0.5)).astype(BF16)
        q_ref[...] = q
        heads = two_heads(q)
        qseg = jnp.concatenate([qseg_ref[seq], qseg_ref[seq]], axis=1)

        def one_slot(slot):
            kv = (dot(u[slot][...], wkv_ref[...], NN) + bias).astype(BF16)
            kv_ref[slot] = kv
            mask = kseg_ref[seq, slot * tokens : (slot + 1) * tokens] == qseg
            scores = jnp.where(mask, dot(kv[:, :128], heads, NT), -1e30)
            best = jnp.max(scores, axis=0, keepdims=True)
            if slot != OWN:
                old = top[...]
                best = jnp.maximum(best, old)
            expo = jnp.exp(scores - best)
            sums = jnp.sum(expo, axis=0, keepdims=True)
            part = dot(kv[:, 128:], expo.astype(BF16), TN)
            if slot != OWN:
                shrink = jnp.exp(old - best)
                sums = sums + total[...] * shrink
                part = part + acc[...] * shrink
            top[...] = best
            total[...] = sums
            acc[...] = part

        one_slot(OWN)
        for slot in SLOT_ORDER[1:]:
            pl.when(need_ref[seq * SLOTS + slot] > 0)(lambda slot=slot: one_slot(slot))
        mixed_ref[...] = own_lanes(acc[...] / total[...], tokens).astype(BF16)
        lse_ref[0] = top[...] + jnp.log(total[...])

    return pl.pallas_call(
        kernel,
        cost_estimate=busy(16),
        grid_spec=pltpu.PrefetchScalarGridSpec(
            num_scalar_prefetch=1,
            grid=(pairs,),
            in_specs=[whole()] * SLOTS
            + [
                pl.BlockSpec((width, 256), lambda p, n: (0, p)),
                pl.BlockSpec((width, 128), lambda p, n: (0, 2 * pairs + p)),
                pl.BlockSpec((1, 128), lambda p, n: (0, p)),
                pl.BlockSpec((1, 128), lambda p, n: (0, p)),
                whole(),
                whole(),
            ],
            out_specs=[
                pl.BlockSpec((tokens, 128), lambda p, n: (0, p)),
                pl.BlockSpec((SLOTS, tokens, 256), lambda p, n: (0, 0, p)),
                pl.BlockSpec((tokens, 128), lambda p, n: (0, p)),
                pl.BlockSpec((1, 1, 2 * tokens), lambda p, n: (p, 0, 0)),
            ],
            scratch_shapes=[
                pltpu.VMEM((1, 2 * tokens), F32),
                pltpu.VMEM((1, 2 * tokens), F32),
                pltpu.VMEM((128, 2 * tokens), F32),
            ],
        ),
        out_shape=(
            jax.ShapeDtypeStruct((tokens, half), BF16),
            jax.ShapeDtypeStruct((SLOTS, tokens, width), BF16),
            jax.ShapeDtypeStruct((tokens, half), BF16),
            jax.ShapeDtypeStruct((pairs, 1, 2 * tokens), F32),
        ),
    )(need, *window, weights, weights, query_bias, value_bias, query_ids, key_ids)


def attend_back(window, weights, out_rows, kept, grad_rows, query_ids, key_ids, need):
    tokens, width = window[0].shape
    half = width // 2
    pairs = half // 128
    blocks = 2 * SLOTS

    def kernel(need_ref, *refs):
        u = refs[:blocks]
        wkv_ref, wq_ref, wo_ref, *rest = refs[blocks:]
        saved_refs = (rest[:4], rest[4:8])
        (
            g_ref, qseg_ref, kseg_ref,
            dw_ref, dwo_ref, dbq_ref, dbv_ref, own_ref, peer_ref,
            probs_ref, grads_ref, inner_ref, acc, gkv, gq, u_all, sems,
        ) = rest[8:]
        pair = pl.program_id(0)
        copies = [
            pltpu.make_async_copy(u[i], u_all.at[pl.ds(i * tokens, tokens)], sems.at[i]) for i in range(blocks)
        ]

        @pl.when(pair == 0)
        def _():
            for c in copies:
                c.start()

        mixed = [refs_of[2][...] for refs_of in saved_refs]
        dwo_ref[...] = (dot(mixed[0], g_ref[:tokens], TN) + dot(mixed[1], g_ref[tokens:], TN)).astype(BF16)
        kv_cols = pl.ds(pl.multiple_of(pair * 256, 256), 256)
        q_cols = pl.ds(pl.multiple_of(pair * 128, 128), 128)
        for seq in range(2):
            q_ref, kv_ref, _, lse_ref = saved_refs[seq]
            gm = dot(g_ref[seq * tokens : (seq + 1) * tokens], wo_ref[...], NT, BF16)
            heads = two_heads(q_ref[...])
            grads = two_heads(gm)
            qseg = jnp.concatenate([qseg_ref[seq], qseg_ref[seq]], axis=1)

            def when(slot, body, seq=seq):
                if slot == OWN:
                    body()
                else:
                    pl.when(need_ref[seq * SLOTS + slot] > 0)(body)

            def probabilities(slot, seq=seq, heads=heads, grads=grads, qseg=qseg, kv_ref=kv_ref, lse_ref=lse_ref):
                mask = kseg_ref[seq, slot * tokens : (slot + 1) * tokens] == qseg
                scores = jnp.where(mask, dot(kv_ref[slot, :, :128], heads, NT), -1e30)
                probs = jnp.exp(scores - lse_ref[0])
                grad_probs = dot(kv_ref[slot, :, 128:], grads, NT)
                part = jnp.sum(probs * grad_probs, axis=0, keepdims=True)
                probs_ref[slot] = probs
                grads_ref[slot] = grad_probs
                inner_ref[...] = part if slot == OWN else inner_ref[...] + part

            def gradients(slot, seq=seq, heads=heads, grads=grads, kv_ref=kv_ref):
                probs = probs_ref[slot]
                grad_scores = (probs * (grads_ref[slot] - inner_ref[...])).astype(BF16)
                part = dot(kv_ref[slot, :, :128], grad_scores, TN)
                acc[...] = part if slot == OWN else acc[...] + part
                gk = dot(grad_scores, heads, NN, BF16)
                gv = dot(probs.astype(BF16), grads, NN, BF16)
                at = (seq * SLOTS + slot) * tokens
                gkv[at : at + tokens, kv_cols] = jnp.concatenate([gk, gv], axis=1)

            for slot in SLOT_ORDER:
                when(slot, lambda slot=slot: probabilities(slot))
            for slot in SLOT_ORDER:
                when(slot, lambda slot=slot: gradients(slot))
                if slot != OWN:

                    @pl.when(need_ref[seq * SLOTS + slot] == 0)
                    def _(at=(seq * SLOTS + slot) * tokens):
                        gkv[at : at + tokens, kv_cols] = jnp.zeros((tokens, 256), BF16)

            gq[seq * tokens : (seq + 1) * tokens, q_cols] = own_lanes(acc[...], tokens).astype(BF16) * (HD**-0.5)

        @pl.when(pair == pairs - 1)
        def _():
            for c in copies:
                c.wait()
            dw_ref[:, :width] = dot(u_all[...], gkv[...], TN, BF16)
            dw_ref[:, width:] = (
                dot(u_all[OWN * tokens : (OWN + 1) * tokens], gq[:tokens], TN)
                + dot(u_all[(SLOTS + OWN) * tokens : (SLOTS + OWN + 1) * tokens], gq[tokens:], TN)
            ).astype(BF16)
            dbq_ref[...] = jnp.sum(gq[...].astype(F32), axis=0, keepdims=True)
            for p in range(pairs):
                values = gkv[:, 256 * p + 128 : 256 * p + 256].astype(F32)
                dbv_ref[:, 128 * p : 128 * p + 128] = jnp.sum(values, axis=0, keepdims=True)
            for seq, out in ((0, own_ref), (1, peer_ref)):
                for slot in range(SLOTS):
                    at = (seq * SLOTS + slot) * tokens

                    def part(at=at):
                        return dot(gkv[at : at + tokens], wkv_ref[...], NT)

                    if slot == OWN:
                        own = dot(gq[seq * tokens : (seq + 1) * tokens], wq_ref[...], NT)
                        out[slot] = (part() + own).astype(BF16)
                        continue
                    wanted = need_ref[seq * SLOTS + slot] > 0

                    @pl.when(wanted)
                    def _(slot=slot, out=out, part=part):
                        out[slot] = part().astype(BF16)

                    @pl.when(jnp.logical_not(wanted))
                    def _(slot=slot, out=out):
                        out[slot] = jnp.zeros((tokens, width), BF16)

    saved_specs = [
        pl.BlockSpec((tokens, 128), lambda p, n: (0, p)),
        pl.BlockSpec((SLOTS, tokens, 256), lambda p, n: (0, 0, p)),
        pl.BlockSpec((tokens, 128), lambda p, n: (0, p)),
        pl.BlockSpec((1, 1, 2 * tokens), lambda p, n: (p, 0, 0)),
    ]
    full = lambda *shape: pl.BlockSpec(shape, lambda p, n: (0,) * len(shape))
    return pl.pallas_call(
        kernel,
        cost_estimate=busy(40),
        grid_spec=pltpu.PrefetchScalarGridSpec(
            num_scalar_prefetch=1,
            grid=(pairs,),
            in_specs=[whole(pl.ANY)] * blocks
            + [full(width, width), pl.BlockSpec((width, half), lambda p, n: (0, 2)), pl.BlockSpec((128, width), lambda p, n: (p, 0))]
            + saved_specs * 2
            + [whole(), whole(), whole()],
            out_specs=[
                full(width, width + half),
                pl.BlockSpec((128, width), lambda p, n: (p, 0)),
                full(1, half),
                full(1, half),
                full(SLOTS, tokens, width),
                full(SLOTS, tokens, width),
            ],
            scratch_shapes=[
                pltpu.VMEM((SLOTS, tokens, 2 * tokens), F32),
                pltpu.VMEM((SLOTS, tokens, 2 * tokens), F32),
                pltpu.VMEM((1, 2 * tokens), F32),
                pltpu.VMEM((128, 2 * tokens), F32),
                pltpu.VMEM((blocks * tokens, width), BF16),
                pltpu.VMEM((2 * tokens, half), BF16),
                pltpu.VMEM((blocks * tokens, width), BF16),
                pltpu.SemaphoreType.DMA((blocks,)),
            ],
        ),
        out_shape=(
            jax.ShapeDtypeStruct((width, width + 2 * half), BF16),
            jax.ShapeDtypeStruct((half, width), BF16),
            jax.ShapeDtypeStruct((1, half), F32),
            jax.ShapeDtypeStruct((1, half), F32),
            jax.ShapeDtypeStruct((SLOTS, tokens, width), BF16),
            jax.ShapeDtypeStruct((SLOTS, tokens, width), BF16),
        ),
    )(need, *window, weights, weights, out_rows, *kept[0], *kept[1], grad_rows, query_ids, key_ids)


def with_output_gradient(grads, mine, theirs, core):
    width, columns = grads.shape
    half = width // 2

    def kernel(core_ref, _, mine_ref, theirs_ref, out_ref):
        at = pl.multiple_of(core_ref[0] * half, 128)
        out_ref[pl.ds(at, half)] = mine_ref[...]
        out_ref[pl.ds(pl.multiple_of((1 - core_ref[0]) * half, 128), half)] = theirs_ref[...]

    return pl.pallas_call(
        kernel,
        cost_estimate=busy(2),
        grid_spec=pltpu.PrefetchScalarGridSpec(
            num_scalar_prefetch=1,
            grid=(1,),
            in_specs=[
                whole(pl.ANY),
                pl.BlockSpec((half, half), lambda i, c: (0, c[0])),
                pl.BlockSpec((half, half), lambda i, c: (0, 0)),
            ],
            out_specs=pl.BlockSpec((width, half), lambda i, c: (0, 3)),
        ),
        out_shape=jax.ShapeDtypeStruct((width, columns), BF16),
        input_output_aliases={1: 0},
    )(core.reshape(1).astype(jnp.int32), grads, mine, theirs)


def feed_gradient(settled, grad_inner, activated, grad_outer):
    rows, width = settled[0].shape
    wide = activated[0].shape[1]

    def kernel(*refs):
        (a0, a1, gi0, gi1, b0, b1, go0, go1, out_ref, sum_ref) = refs
        i = pl.program_id(0)

        @pl.when(i == 0)
        def _():
            out_ref[...] = (dot(a0[...], gi0[...], TN) + dot(a1[...], gi1[...], TN)).astype(BF16)
            total = jnp.sum(gi0[...].astype(F32), axis=0, keepdims=True)
            sum_ref[...] = total + jnp.sum(gi1[...].astype(F32), axis=0, keepdims=True)

        @pl.when(i == 1)
        def _():
            out_ref[...] = (dot(b0[...], go0[...], TN) + dot(b1[...], go1[...], TN)).astype(BF16)

    return pl.pallas_call(
        kernel,
        cost_estimate=busy(6),
        grid=(2,),
        in_specs=[whole()] * 8,
        out_specs=[pl.BlockSpec((width, wide), lambda i: (0, i)), pl.BlockSpec((1, wide), lambda i: (0, 0))],
        out_shape=[jax.ShapeDtypeStruct((width, 2 * wide), BF16), jax.ShapeDtypeStruct((1, wide), F32)],
    )(*settled, *grad_inner, *activated, *grad_outer)


def vector_grad_rows(grads, core, x, n):
    width = grads[0][2].shape[1]
    half = width // 2
    per = width // n
    wide = grads[0][8].shape[1]
    quarter = wide // n
    if per % 128 or quarter % 128:
        rows = []
        for g in grads:
            halves = [lax.dynamic_update_slice(jnp.zeros((1, width), F32), v, (0, core * half)) for v in g[:2]]
            b1 = jnp.zeros((n, 4, quarter), F32)
            b1 = lax.dynamic_update_slice(b1, g[8].reshape(n, 1, quarter), (0, core * 2 + x, 0))
            rows.append(
                jnp.concatenate([v.reshape(n, per) for v in halves + list(g[2:8])] + [b1.reshape(n, -1)], axis=1)
            )
        block = jnp.stack(rows, axis=1)
        return jnp.pad(block, ((0, 0), (0, 16 - LAYERS), (0, 2048 - block.shape[2])))

    def kernel(sel_ref, *refs):
        out = refs[-1]
        out[...] = jnp.zeros_like(out)
        core_at = sel_ref[0] * (n // 2)
        for l in range(LAYERS):
            mine = refs[9 * l : 9 * l + 9]
            for i in range(2):
                for t in range(n // 2):
                    out[core_at + t, l : l + 1, i * per : (i + 1) * per] = mine[i][:, t * per : (t + 1) * per]
            for i in range(2, 8):
                for t in range(n):
                    out[t, l : l + 1, i * per : (i + 1) * per] = mine[i][:, t * per : (t + 1) * per]
            at = pl.multiple_of(8 * per + sel_ref[1] * quarter, 128)
            for t in range(n):
                out[t, l : l + 1, pl.ds(at, quarter)] = mine[8][:, t * quarter : (t + 1) * quarter]

    return pl.pallas_call(
        kernel,
        cost_estimate=busy(2),
        in_specs=[whole(pltpu.SMEM)] + [whole()] * (9 * LAYERS),
        out_specs=whole(),
        out_shape=jax.ShapeDtypeStruct((n, 16, 2048), F32),
    )(jnp.stack([core, core * 2 + x]).astype(jnp.int32), *[v for g in grads for v in g])


def into_layer(kernel, name, layer, before, shapes, blocks, sel, inputs, in_specs, grid):
    held = [] if before is None else list(before)

    def body(sel_ref, *refs):
        kernel(sel_ref, *refs[len(held) :])

    return pl.pallas_call(
        body,
        cost_estimate=busy(4),
        name=name,
        grid_spec=pltpu.PrefetchScalarGridSpec(
            num_scalar_prefetch=1,
            grid=grid,
            in_specs=[whole(pl.ANY)] * len(held) + in_specs,
            out_specs=blocks,
        ),
        out_shape=shapes,
        input_output_aliases={1 + i: i for i in range(len(held))},
    )(sel, *held, *inputs)


def finish_feed(layer, before, pieces, core, x):
    per = pieces[0].shape[0]
    wide = width = pieces[0].shape[1] // 2
    n = lax.axis_size("ctx")
    quarter = wide // n
    places = jnp.stack([core * 2 + x, core * 2 + 1 - x, (1 - core) * 2 + x, (1 - core) * 2 + 1 - x]).astype(jnp.int32)
    shapes = (
        jax.ShapeDtypeStruct((LAYERS, per, 4 * wide), F32),
        jax.ShapeDtypeStruct((LAYERS, 4 * per, width), F32),
    )
    if quarter % 128:
        first = jnp.zeros((4, per, n, quarter), F32)
        second = jnp.zeros((4, per, width), F32)
        for i, piece in enumerate(pieces):
            piece = piece.astype(F32)
            first = lax.dynamic_update_index_in_dim(first, piece[:, :wide].reshape(per, n, quarter), places[i], 0)
            second = lax.dynamic_update_index_in_dim(second, piece[:, wide:], places[i], 0)
        first = jnp.transpose(first, (1, 2, 0, 3)).reshape(1, per, 4 * wide)
        second = second.reshape(1, 4 * per, width)
        base = [jnp.zeros(s.shape, F32) for s in shapes] if before is None else before
        return tuple(lax.dynamic_update_slice(b, v, (layer, 0, 0)) for b, v in zip(base, (first, second)))

    def kernel(sel_ref, a, b, c, d, first, second):
        for i, ref in enumerate((a, b, c, d)):
            at = pl.multiple_of(sel_ref[i] * quarter, 128)
            for j in range(n):
                cols = pl.ds(4 * j * quarter + at, quarter)
                first[0, :, cols] = ref[:, j * quarter : (j + 1) * quarter].astype(F32)
            second[0, pl.ds(pl.multiple_of(sel_ref[i] * per, 8), per), :] = ref[:, wide:].astype(F32)

    return into_layer(
        kernel, "finish_feed", layer, before, shapes,
        tuple(pl.BlockSpec((1,) + s.shape[1:], lambda i, s: (layer, 0, 0)) for s in shapes),
        places, pieces, [whole()] * 4, (1,),
    )


def finish_attention(layer, before, sums, core, per):
    rows, columns = sums[0].shape
    half = columns // 4
    pairs = half // 128
    shape = jax.ShapeDtypeStruct((LAYERS, per, 2 * half), F32)
    more = rows > per

    def kernel(sel_ref, a, b, c, d, q_out, k_out, v_out, o_out, *extra):
        for i, (low, came) in enumerate(((a, b), (c, d))):
            at = pl.multiple_of((sel_ref[0] if i == 0 else 1 - sel_ref[0]) * half, 128)

            def part(start, size, low=low, came=came):
                cols = slice(start, start + size)
                return low[:per, cols].astype(F32) + came[:per, cols].astype(F32)

            for p in range(pairs):
                k_out[0, :, pl.ds(at + 128 * p, 128)] = part(256 * p, 128)
                v_out[0, :, pl.ds(at + 128 * p, 128)] = part(256 * p + 128, 128)
            q_out[0, :, pl.ds(at, half)] = part(2 * half, half)
            o_out[0, :, pl.ds(at, half)] = part(3 * half, half)
        if more:
            first = a[per:].astype(F32) + b[per:].astype(F32)
            extra[0][...] = first + (c[per:].astype(F32) + d[per:].astype(F32))

    block = pl.BlockSpec((1, per, 2 * half), lambda i, s: (layer, 0, 0))
    shapes, blocks = (shape,) * 4, (block,) * 4
    if more:
        shapes += (jax.ShapeDtypeStruct((rows - per, columns), F32),)
        blocks += (pl.BlockSpec((rows - per, columns), lambda i, s: (0, 0)),)
    return into_layer(
        kernel, "finish_attention", layer, before, shapes, blocks,
        core.reshape(1).astype(jnp.int32), sums, [whole()] * 4, (1,),
    )


def normalize(operand, gain, shift):
    centered = operand - jnp.mean(operand, axis=-1, keepdims=True)
    spread = jnp.mean(centered * centered, axis=-1, keepdims=True)
    return centered * lax.rsqrt(spread + 1e-05) * gain + shift


def normalize_back(operand, gain, grad):
    centered = operand - jnp.mean(operand, axis=-1, keepdims=True)
    spread = jnp.mean(centered * centered, axis=-1, keepdims=True)
    inverse = lax.rsqrt(spread + 1e-05)
    unit = centered * inverse
    scaled = grad * gain
    out = inverse * (
        scaled
        - jnp.mean(scaled, axis=-1, keepdims=True)
        - unit * jnp.mean(scaled * unit, axis=-1, keepdims=True)
    )
    return out, jnp.sum(grad * unit, axis=0), jnp.sum(grad, axis=0)


def column_sums(operand):
    return jnp.sum(operand.astype(F32), axis=0)


def shifts(n, by):
    return [(i, i + by) for i in range(n) if 0 <= i + by < n]


def slot_ids(group_ids, tokens, n):
    ctx = lax.axis_index("ctx")
    per = SEQ // tokens
    odd = ctx % 2 == 1
    blocks = [ctx - 2, ctx ^ 1, ctx, jnp.where(odd, ctx + 1, ctx - 1), ctx + 2]
    out = []
    for block in blocks:
        inside = (block >= 0) & (block < n) & (block // per == ctx // per)
        start = jnp.clip(block, 0, n - 1) * tokens
        out.append(jnp.where(inside, lax.dynamic_slice_in_dim(group_ids, start, tokens), -1))
    return jnp.stack(out)


def local(
    hidden_in,
    segment_ids,
    query_weight,
    query_bias,
    key_weight,
    value_weight,
    value_bias,
    output_weight,
    output_bias,
    first_gain,
    first_shift,
    inner_weight,
    inner_bias,
    outer_weight,
    outer_bias,
    second_gain,
    second_shift,
    cotangent,
):
    tokens, width = hidden_in.shape
    n = lax.axis_size("ctx")
    ctx = lax.axis_index("ctx")
    dp = lax.axis_index("dp")
    core = dp % 2
    x = dp // 2
    half = width // 2
    ff = inner_weight.shape[2]
    per = width // n
    quarter = ff // (4 * n)
    wide = ff // 4
    ring = Ring(n)
    beats = Beats()
    odd = ctx % 2 == 1
    beside_pairs = [(i, i ^ 1) for i in range(n)]
    core_index = core.reshape(1).astype(jnp.int32)

    vectors = [
        query_bias, value_bias, output_bias, first_gain, first_shift,
        outer_bias, second_gain, second_shift, inner_bias,
    ]
    vector_size = 8 * per + ff // n
    matrices = (query_weight, key_weight, value_weight, output_weight)

    extra = vector_rows(vectors)
    packs = [
        pack_layer(matrices, inner_weight, outer_weight, layer, core, x, extra if layer == 0 else None)
        for layer in range(LAYERS)
    ]
    attn_in = Gather(ring, lambda: packs[0][0], 1)
    for sign in (1, -1):
        beats.start(attn_in.stream(sign))

    arrived = {}

    def native_gathers():
        feed = yield packs[0][1]
        feed = yield feed
        for name, pack, held_beats in (("f0", feed, 3), ("a1", packs[1][0], 2), ("f1", packs[1][1], 3)):
            arrived[name] = yield Hold(lax.all_gather(pack, "ctx", axis=0, tiled=True), held_beats)

    beats.start(native_gathers())

    watch, watch_until = beats.beat, beats.until

    own_ids = segment_ids.reshape(-1)
    key_ids = jnp.stack([slot_ids(own_ids, tokens, n), slot_ids(core_swap(own_ids), tokens, n)])
    query_ids = key_ids[:, OWN]
    low, high = jnp.min(query_ids, axis=1), jnp.max(query_ids, axis=1)
    need = (jnp.max(key_ids, axis=2) >= low[:, None]) & (jnp.min(key_ids, axis=2) <= high[:, None])
    need = need.astype(jnp.int32).reshape(-1)
    query_ids = query_ids.reshape(2, 1, tokens)
    key_ids = key_ids.reshape(2, SLOTS * tokens, 1)

    def both(value):
        return jnp.concatenate([value, core_swap(value)], axis=0)

    def far(value):
        beyond = x_swap(value)
        return jnp.concatenate([beyond, core_swap(beyond)], axis=0)

    def pair_sum(partial):
        return partial[:tokens] + core_swap(partial[tokens:].astype(BF16)).astype(F32)

    def sum_group(partial_near, partial_far):
        beyond = x_swap(pair_sum(partial_far).astype(BF16)).astype(F32)
        return pair_sum(partial_near) + beyond

    def sum_cores(partial):
        return partial[:tokens] + core_swap(partial[tokens:])

    def window_streams(own, sink):
        def behind():
            sink["behind"] = yield lax.ppermute(own, "ctx", shifts(n, 2))

        def ahead():
            sink["ahead"] = yield lax.ppermute(own, "ctx", shifts(n, -2))

        def side():
            sink["beside"] = yield lax.ppermute(own, "ctx", beside_pairs)
            send = jnp.where(odd, sink["behind"], sink["ahead"])
            sink["across"] = yield lax.ppermute(send, "ctx", beside_pairs)

        for stream in (behind(), ahead(), side()):
            beats.start(stream)

    def window_of(own, sink):
        mine = [sink["behind"], sink["beside"], own, sink["across"], sink["ahead"]]
        return mine + [core_swap(block) for block in mine]

    hidden = hidden_in.astype(F32)
    rounded = hidden_in
    sink = {}
    window_streams(rounded, sink)
    saved = []
    weights = []
    vector_block = None
    for layer in range(LAYERS):
        hidden, rounded = watch_until(
            lambda sink=sink, layer=layer: attn_in.ready() and "across" in sink and (layer == 0 or "a1" in arrived),
            hidden, rounded,
        )
        if layer == 0:
            chunks, owners = attn_in.chunks()
            w_attn, vector_block = assemble(chunks, owners, [(per, 0, 0, 4 * half), (16, per // 16, 0, 4 * half)])
            w_attn = w_attn.reshape(width, 4 * half)
        else:
            w_attn = arrived["a1"]
        window = window_of(rounded, sink)
        out_half = w_attn[:, 3 * half :]
        theirs = core_swap(lax.dynamic_slice_in_dim(out_half, (1 - core) * half, half, 0))
        wo = ordered(core, lax.dynamic_slice_in_dim(out_half, core * half, half, 0), theirs, 1)

        block = vector_block[:, layer, :vector_size].astype(F32)
        flat_vectors = [block[:, i * per : (i + 1) * per].reshape(1, -1) for i in range(8)]
        b1 = lax.dynamic_index_in_dim(block[:, 8 * per :].reshape(n, 2, 2, quarter), core, 1, keepdims=False)
        b1 = lax.dynamic_index_in_dim(b1, x, 1, keepdims=False).reshape(1, -1)
        bq, bv = [lax.dynamic_slice_in_dim(v, core * half, half, 1) for v in flat_vectors[:2]]
        bo, g1, c1, b2, g2, c2 = flat_vectors[2:]

        first = attend(window[:SLOTS], w_attn, bq, bv, query_ids, key_ids, need, 0)
        (hidden, w_attn, *first) = watch(hidden, w_attn, *first)
        second = attend(window[SLOTS:], w_attn, bq, bv, query_ids, key_ids, need, 1)
        (hidden, *second) = watch(hidden, *second)
        mixed = jnp.concatenate([first[2], second[2]], axis=0)
        first_sum = hidden + (sum_cores(dot(mixed, wo, NN)) + bo)
        settled = normalize(first_sum, g1, c1)
        settled_low = settled.astype(BF16)
        settled_rows = (both(settled_low), far(settled_low))
        name = "f" + str(layer)
        settled, settled_low = watch_until(lambda name=name: name in arrived, settled, settled_low)
        w_feed = arrived[name]

        def feed_in(rows, w_feed=w_feed, b1=b1):
            inner = dot(rows, w_feed[:, :wide], NN) + b1
            cdf = (1.0 + lax.erf(inner * (0.5**0.5))) * 0.5
            slope = cdf + inner * jnp.exp(-0.5 * inner * inner) * (0.5 / jnp.pi) ** 0.5
            return (inner * cdf).astype(BF16), slope

        act_near, slope_near = feed_in(settled_rows[0])
        act_far, slope_far = feed_in(settled_rows[1])
        partial_far = dot(act_far, w_feed[:, wide:], NN)
        partial_near = dot(act_near, w_feed[:, wide:], NN)
        second_sum = settled + (sum_group(partial_near, partial_far) + b2)
        slope = (slope_near, slope_far)
        activated = (act_near, act_far)
        hidden = normalize(second_sum, g2, c2)
        weights.append((w_attn, wo, w_feed, g1, g2))
        saved.append((window, (first, second), first_sum, settled_rows, slope, activated, second_sum))
        if layer + 1 < LAYERS:
            rounded = hidden.astype(BF16)
            sink = {}
            window_streams(rounded, sink)
    output = hidden.astype(BF16)

    jobs = []

    def step(*state):
        state = beats.beat(*state)
        for job in list(jobs):
            if job[0].ready():
                job[1](job[0].total())
                jobs.remove(job)
        return state

    held = {"feed": None, "attn": None}
    tail_vectors = []

    def shared(low_sum, done):
        mirror = core_swap(low_sum)

        def stream():
            came = yield x_swap(low_sum)
            done([low_sum, came, mirror, core_swap(came)])

        beats.start(stream())

    def feed_done(low_sum, layer):
        def stream():
            mirror = core_swap(low_sum)
            other = yield x_swap(low_sum)
            held["feed"] = finish_feed(layer, held["feed"], [low_sum, other, mirror, core_swap(other)], core, x)
            beats.keep(held, "feed")

        beats.start(stream())

    def attention_done(sums, layer):
        parts = finish_attention(layer, held["attn"], sums, core, per)
        held["attn"] = parts[:4]
        beats.keep(held, "attn")
        tail_vectors.extend(parts[4:])

    vector_grads = [None] * LAYERS
    grad = cotangent.astype(F32)

    def native(value, held_beats, done):
        def stream():
            done((yield Hold(lax.psum_scatter(value, "ctx", scatter_dimension=0, tiled=True), held_beats)))

        beats.start(stream())

    for layer in reversed(range(LAYERS)):
        w_attn, wo, w_feed, g1, g2 = weights[layer]
        window, kept, first_sum, settled_rows, slope, activated, second_sum = saved[layer]
        last = layer == 0
        grad_second, d_g2, d_c2 = normalize_back(second_sum, g2, grad)
        go = grad_second.astype(BF16)
        go_rows = (both(go), far(go))
        d_b2 = column_sums(go)
        gi = [(s * dot(rows, w_feed[:, wide:], NT)).astype(BF16) for s, rows in zip(slope, go_rows)]
        partial_far = dot(gi[1], w_feed[:, :wide], NT)
        partial_near = dot(gi[0], w_feed[:, :wide], NT)
        gset = grad_second + sum_group(partial_near, partial_far)
        d_feed, d_b1 = feed_gradient(settled_rows, gi, activated, go_rows)
        gset, d_feed = step(gset, d_feed)
        native(d_feed, 3 if not last else 5, lambda total, layer=layer: feed_done(total, layer))
        grad_first, d_g1, d_c1 = normalize_back(first_sum, g1, gset)
        gb = grad_first.astype(BF16)
        gb_rows = both(gb)
        d_bo = column_sums(gb)
        grad_first, gb_rows = step(grad_first, gb_rows)
        d_attn, d_wo, d_bq, d_bv, du_own, du_peer = attend_back(
            window, w_attn, wo, kept, gb_rows, query_ids, key_ids, need
        )
        give = lax.dynamic_slice_in_dim(d_wo, (1 - core) * half, half, 1)
        d_attn = with_output_gradient(d_attn, d_wo, core_swap(give), core)
        parts = du_own.astype(F32) + core_swap(du_peer).astype(F32)
        grad_first, d_attn, parts = step(grad_first, d_attn, parts)
        back = {}

        def send(name, value, pairs, back=back):
            def stream():
                back[name] = (yield lax.ppermute(value.astype(BF16), "ctx", pairs)).astype(F32)

            beats.start(stream())

        send("across", parts[3], beside_pairs)
        send("beside", parts[1], beside_pairs)
        vector_grads[layer] = (
            d_bq, d_bv, d_bo[None], d_g1[None], d_c1[None], d_b2[None], d_g2[None], d_c2[None],
            d_b1,
        )
        if last:
            tail = vector_grad_rows(vector_grads, core, x, n)

            def attention_part(t, d_attn=d_attn.reshape(n, per, -1)):
                part = lax.dynamic_index_in_dim(d_attn, t, 0, keepdims=False).astype(F32)
                below = lax.dynamic_index_in_dim(tail, t, 0, keepdims=False)
                return jnp.concatenate([part, below], axis=0)

            def attention_ring_done(total):
                shared(total.astype(BF16), lambda sums: attention_done(sums, 0))

            attention_ring = Scatter(ring, attention_part, 1)
            jobs.append((attention_ring, attention_ring_done))
            beats.start(attention_ring.stream(1))
            beats.start(attention_ring.stream(-1))
        while "across" not in back:
            grad_first, parts, d_attn = step(grad_first, parts, d_attn)
        send("ahead", parts[0] + jnp.where(odd, back["across"], 0.0), shifts(n, -2))
        send("behind", parts[4] + jnp.where(odd, 0.0, back["across"]), shifts(n, 2))
        own_part, d_attn = step(grad_first + parts[2] + back["beside"], d_attn)
        grad = own_part + back["ahead"] + back["behind"]
        if not last:
            native(d_attn, 3, lambda total: shared(total, lambda sums: attention_done(sums, 1)))
    while beats.streams or jobs:
        step()

    fields = tail_vectors[0][:LAYERS, :vector_size]
    own_vectors = [fields[:, i * per : (i + 1) * per] for i in range(8)] + [fields[:, 8 * per :]]
    d_bq, d_bv, d_bo, d_g1, d_c1, d_b2, d_g2, d_c2, d_b1 = own_vectors
    dq, dk, dv, do = held["attn"]
    return (
        output,
        grad.astype(BF16),
        dq, d_bq, dk, dv, d_bv, do, d_bo, d_g1, d_c1, held["feed"][0], d_b1, held["feed"][1], d_b2, d_g2, d_c2,
    )


def solution(mesh):
    tokens = P(("dp", "ctx"), None)
    matrix = P(None, "ctx", None)
    vector = P(None, "ctx")
    params = (
        matrix, vector, matrix, matrix, vector, matrix, vector, vector,
        vector, matrix, vector, matrix, vector, vector, vector,
    )
    return jax.shard_map(
        local,
        mesh=mesh,
        in_specs=(tokens, P("dp", None, None)) + params + (tokens,),
        out_specs=(tokens, tokens) + params,
        check_vma=False,
    )
```
